32 devices in a mesh: groups: 2 (over x), rows: 16 (over z, y, core).
Axes of the slice: x: 2, y: 2, z: 4, core: 2. Of those that a mesh axis runs over, the one named last changes fastest.
Arguments:
- latent: bfloat16 [256, 256, 320], P(('groups', 'rows')), parts along dimension 0, may hold values from -170 to 170
- crop_shift: int32 [4], P('groups'), parts along dimension 0, may hold values from 0 to 31
- dilation_shift: int32 [4], P('groups'), parts along dimension 0, may hold values from 0 to 31
- local_gain: float32 [320], replicated, may hold values from 0.5 to 1.5
- local_bias: float32 [320], replicated, may hold values from -3 to 3
- local_kernel: bfloat16 [3, 3, 320, 320], replicated, may hold values from -0.109375 to 0.109375
- local_offset: float32 [320], replicated, may hold values from -2 to 2
- global_gain: float32 [320], replicated, may hold values from 0.5 to 1.5
- global_bias: float32 [320], replicated, may hold values from -3 to 3
- global_kernel: bfloat16 [3, 3, 320, 320], replicated, may hold values from -0.109375 to 0.109375
- global_offset: float32 [320], replicated, may hold values from -2 to 2
Outputs:
- update: bfloat16 [256, 256, 320], P(('groups', 'rows')), parts along dimension 0
The draws below stay inside these ranges and needn't reach their ends.
There are 2 independent parts, one for each index of `groups`. The reference program is written for one: setup_inputs(seed, part) draws one part's arguments, and reference() takes and returns one part's arrays. A program takes and returns all parts, laid end to end along the dimension named above; an argument that names none is the same for every part. Nothing has to cross between parts.
All inputs are finite; a program needn't handle non-finite values.
Results may differ from the reference program's by a relative error of at most 0.0053.
Values may be sent and summed in bfloat16 or wider, within the bound.
No kernel may reach another device: no remote copies, remote signals or barrier semaphores. Data moves between devices by JAX's collectives and lax.ppermute only.
A program may use at most 128 MiB of HBM per device.

```python
import math
import jax
import jax.numpy as jnp
from jax import lax

LATENT_CHANNELS = 320
NORM_GROUPS = 32
DILATION_COLUMNS = 8
SUBIMAGE_COLUMNS = 32
CROP = 32
DILATION_ROWS = 2
SUBIMAGE_ROWS = 64
LATENT_COLUMNS = 256
LATENT_ROWS = 128


def draw_latent(key, part):
    key_base = jax.random.fold_in(key, 11)
    key_rows = jax.random.fold_in(key, 12)
    key_cols = jax.random.fold_in(key, 13)
    row_pos = jnp.arange(LATENT_ROWS, dtype=jnp.float32)
    row_scale = 3.0 ** (row_pos / LATENT_ROWS) * jnp.exp(jax.random.uniform(key_rows, (LATENT_ROWS,), minval=0.0, maxval=math.log(3.0)))
    col_scale = jnp.exp(jax.random.uniform(key_cols, (LATENT_COLUMNS,), minval=0.0, maxval=math.log(3.0)))
    base_values = jnp.clip(jax.random.normal(key_base, (LATENT_ROWS, LATENT_COLUMNS, LATENT_CHANNELS)), -6.0, 6.0)
    return (base_values * row_scale[:, None, None] * col_scale[None, :, None]).astype(jnp.bfloat16)


def normal_values(rng, dims, deviation, bound, kind=jnp.bfloat16):
    array = jax.random.normal(rng, dims, jnp.float32) * deviation
    return jnp.minimum(jnp.maximum(array, -bound), bound).astype(kind)


def setup_inputs(seed: int = 0, part: int = 0) -> dict:
    keys = jax.random.split(jax.random.key(seed), 12)
    part_keys = jax.random.split(jax.random.fold_in(keys[11], part), 12)
    return {
        "latent": draw_latent(jax.random.fold_in(jax.random.fold_in(keys[11], part), 71), part),
        "crop_shift": jax.random.randint(part_keys[1], (2,), 0, CROP).astype(jnp.int32),
        "dilation_shift": jax.random.randint(part_keys[2], (2,), 0, 32).astype(jnp.int32),
        "local_gain": jnp.clip(1.0 + 0.1 * jax.random.normal(keys[3], (LATENT_CHANNELS,), jnp.float32), 0.5, 1.5),
        "local_bias": normal_values(keys[4], (LATENT_CHANNELS,), 0.5, 3.0, jnp.float32),
        "local_kernel": normal_values(keys[5], (3, 3, LATENT_CHANNELS, LATENT_CHANNELS), (9 * LATENT_CHANNELS) ** -0.5, 0.109375),
        "local_offset": normal_values(keys[6], (LATENT_CHANNELS,), 0.3, 2.0, jnp.float32),
        "global_gain": jnp.clip(1.0 + 0.1 * jax.random.normal(keys[7], (LATENT_CHANNELS,), jnp.float32), 0.5, 1.5),
        "global_bias": normal_values(keys[8], (LATENT_CHANNELS,), 0.5, 3.0, jnp.float32),
        "global_kernel": normal_values(keys[9], (3, 3, LATENT_CHANNELS, LATENT_CHANNELS), (9 * LATENT_CHANNELS) ** -0.5, 0.109375),
        "global_offset": normal_values(keys[10], (LATENT_CHANNELS,), 0.3, 2.0, jnp.float32),
    }


EPSILON = 1e-05

def group_act(block_list, gain, shift):
    count_b, height_b, width_b, channel_count = block_list.shape
    grouped = block_list.reshape(count_b, height_b, width_b, NORM_GROUPS, channel_count // NORM_GROUPS)
    total = height_b * width_b * (channel_count // NORM_GROUPS)
    mean = lax.optimization_barrier(jnp.sum(grouped, axis=(1, 2, 4), keepdims=True)) / total
    var = lax.optimization_barrier(jnp.sum(grouped * grouped, axis=(1, 2, 4), keepdims=True)) / total - mean * mean
    normed = ((grouped - mean) * lax.rsqrt(var + EPSILON)).reshape(count_b, height_b, width_b, channel_count)
    return jax.nn.silu(normed * gain + shift).astype(jnp.bfloat16)

def conv_blocks(act, kernel, offset):
    result = lax.conv_general_dilated(act.astype(jnp.float32), kernel.astype(jnp.float32), (1, 1), ((1, 1), (1, 1)), dimension_numbers=('NHWC', 'HWIO', 'NHWC'), precision=lax.Precision.HIGHEST)
    return result + offset

def reference(latent, crop_shift, dilation_shift, local_gain, local_bias, local_kernel, local_offset, global_gain, global_bias, global_kernel, global_offset):
    value_tensor = latent.astype(jnp.float32)
    shift_row = crop_shift[0]
    shift_col = crop_shift[1]
    rolled = jnp.roll(value_tensor, (-shift_row, -shift_col), axis=(0, 1))
    block_list = rolled.reshape(LATENT_ROWS // CROP, CROP, LATENT_COLUMNS // CROP, CROP, LATENT_CHANNELS).transpose(0, 2, 1, 3, 4).reshape(-1, CROP, CROP, LATENT_CHANNELS)
    local_out = conv_blocks(group_act(block_list, local_gain, local_bias), local_kernel, local_offset)
    local_out = local_out.reshape(LATENT_ROWS // CROP, LATENT_COLUMNS // CROP, CROP, CROP, LATENT_CHANNELS).transpose(0, 2, 1, 3, 4).reshape(LATENT_ROWS, LATENT_COLUMNS, LATENT_CHANNELS)
    local_out = jnp.roll(local_out, (shift_row, shift_col), axis=(0, 1))
    image_row = jnp.mod(dilation_shift[0], SUBIMAGE_ROWS)
    image_col = jnp.mod(dilation_shift[1], SUBIMAGE_COLUMNS)
    subimages = value_tensor.reshape(SUBIMAGE_ROWS, DILATION_ROWS, SUBIMAGE_COLUMNS, DILATION_COLUMNS, LATENT_CHANNELS).transpose(1, 3, 0, 2, 4).reshape(DILATION_ROWS * DILATION_COLUMNS, SUBIMAGE_ROWS, SUBIMAGE_COLUMNS, LATENT_CHANNELS)
    subimages = jnp.roll(subimages, (-image_row, -image_col), axis=(1, 2))
    global_output = conv_blocks(group_act(subimages, global_gain, global_bias), global_kernel, global_offset)
    global_output = jnp.roll(global_output, (image_row, image_col), axis=(1, 2))
    global_output = global_output.reshape(DILATION_ROWS, DILATION_COLUMNS, SUBIMAGE_ROWS, SUBIMAGE_COLUMNS, LATENT_CHANNELS).transpose(2, 0, 3, 1, 4).reshape(LATENT_ROWS, LATENT_COLUMNS, LATENT_CHANNELS)
    global_low = lax.optimization_barrier(global_output.astype(jnp.bfloat16))
    return (local_out + global_low.astype(jnp.float32)).astype(jnp.bfloat16)
```

```python
import functools

import jax
import jax.numpy as jnp
from jax import lax
from jax.experimental import pallas as pl
from jax.experimental.pallas import tpu as pltpu
from jax.sharding import PartitionSpec as P

NORM_GROUPS = 32
DILATION_COLUMNS = 8
CROP = 32
EPSILON = 1e-05
LANES = 128

BF16 = jnp.bfloat16
F32 = jnp.float32


def split3(value):
    high = value.astype(BF16)
    rest = value - high.astype(F32)
    middle = rest.astype(BF16)
    low = (rest - middle.astype(F32)).astype(BF16)
    return high, middle, low


def exact_dot(value, selector):
    parts = [jnp.dot(part, selector, preferred_element_type=F32) for part in split3(value)]
    return (parts[2] + parts[1]) + parts[0]


def selector_matrix(shape, channel_dim, group_size, offset):
    channel = lax.broadcasted_iota(jnp.int32, shape, channel_dim)
    group = lax.broadcasted_iota(jnp.int32, shape, 1 - channel_dim) - offset
    first = group * group_size
    inside = (channel >= first) & (channel < first + group_size) & (group >= 0)
    inside = inside & (group < NORM_GROUPS)
    return jnp.where(inside, 1.0, 0.0).astype(BF16)


def stats_body(dil_rows, group_size, table, x_ref, out_ref, image_acc, crop_acc):
    step = pl.program_id(0)
    rows, block_cols, channels = x_ref.shape
    split_row = table[0]
    split_col = table[1]
    windows = block_cols // CROP
    kinds = 4 + 2 * dil_rows

    @pl.when(step == 0)
    def _():
        image_acc[...] = jnp.zeros_like(image_acc)

    weights = [jnp.where(r < split_row, 1.0, 0.0).astype(F32) for r in range(rows)]
    for w in range(windows):
        folded = [[None, None] for _ in range(4)]
        for half in range(CROP // 16):
            col = w * CROP + half * 16
            sums = [[None] * dil_rows for _ in range(4)]
            for r in range(rows):
                p = r % dil_rows
                value = x_ref[r, col : col + 16, :].astype(F32)
                first = value * weights[r]
                second = value - first
                items = (first, first * value, second, second * value)
                for k in range(4):
                    sums[k][p] = items[k] if sums[k][p] is None else sums[k][p] + items[k]
            for p in range(dil_rows):
                for k in range(2):
                    image = sums[k][p] + sums[k + 2][p]
                    image_acc[2 * p + k] += image[:8] + image[8:]
            local_col = lax.broadcasted_iota(jnp.int32, (16, channels), 0) + half * 16
            early = local_col < split_col
            for k in range(4):
                total = functools.reduce(lambda a, b: a + b, sums[k])
                head = jnp.where(early, total, 0.0)
                tail = total - head
                for side, part in enumerate((head, tail)):
                    part = part[:8] + part[8:]
                    old = folded[k][side]
                    folded[k][side] = part if old is None else old + part
        for k in range(4):
            for side in range(2):
                crop_acc[2 * k + side, step * windows + w] = folded[k][side]

    @pl.when(step == pl.num_programs(0) - 1)
    def _():
        stack = []
        for k in range(4):
            head = jnp.sum(crop_acc[2 * k], axis=1)
            tail = jnp.sum(crop_acc[2 * k + 1], axis=1)
            count = head.shape[0]
            stack.append(tail + jnp.concatenate([head[1:], head[:1]], axis=0))
        for k in range(2 * dil_rows):
            stack.append(image_acc[k])
        selector = selector_matrix((channels, LANES), 0, group_size, 0)
        compact = exact_dot(jnp.concatenate(stack, axis=0), selector)
        out_ref[...] = jnp.zeros_like(out_ref)
        for t in range(0, kinds, 4):
            tile = None
            for j in range(min(4, kinds - t)):
                part = compact[8 * (t + j) : 8 * (t + j) + 8]
                if j:
                    part = pltpu.roll(part, 32 * j, 1)
                tile = part if tile is None else tile + part
            out_ref[:, 32 * t : 32 * t + LANES] = tile


def strip_statistics(latent, table, dil_rows):
    rows, columns, channels = latent.shape
    block_cols = 64
    width = -(-(4 + 2 * dil_rows) // 4) * LANES
    crops = columns // CROP
    return pl.pallas_call(
        functools.partial(stats_body, dil_rows, channels // NORM_GROUPS),
        out_shape=jax.ShapeDtypeStruct((8, width), F32),
        grid_spec=pltpu.PrefetchScalarGridSpec(
            num_scalar_prefetch=1,
            grid=(columns // block_cols,),
            in_specs=[pl.BlockSpec((rows, block_cols, channels), lambda i, t: (0, i, 0))],
            out_specs=pl.BlockSpec((8, width), lambda i, t: (0, 0)),
            scratch_shapes=[
                pltpu.VMEM((2 * dil_rows, 8, channels), F32),
                pltpu.VMEM((8, crops, 8, channels), F32),
            ],
        ),
        compiler_params=pltpu.CompilerParams(vmem_limit_bytes=16 << 20),
        cost_estimate=pl.CostEstimate(
            flops=12 * latent.size, bytes_accessed=2 * latent.size, transcendentals=0
        ),
        name="strip_statistics",
    )(table, latent)


def packed_width(channels):
    main = channels // LANES * LANES
    left = channels - main
    return main, left, 3 * main + -(-3 * left // LANES) * LANES


def pack_body(local_ref, global_ref, local_out, global_out):
    channels = local_ref.shape[2]
    main, left, width = packed_width(channels)
    for source, target in ((local_ref, local_out), (global_ref, global_out)):
        used = 3 * (main + left)
        if used < width:
            target[used:, :] = jnp.zeros((width - used, width), BF16)
            target[:, width - LANES :] = jnp.zeros((width, LANES), BF16)
        for i in range(3):
            for t in range(3):
                tap = source[i, t]
                rows = slice(i * main, i * main + main)
                cols = slice(t * main, t * main + main)
                target[rows, cols] = tap[:main, :main]
                if left:
                    low_rows = slice(3 * main + i * left, 3 * main + i * left + left)
                    low_cols = slice(3 * main + t * left, 3 * main + t * left + left)
                    target[low_rows, cols] = tap[main:, :main]
                    target[rows, low_cols] = tap[:main, main:]
                    target[low_rows, low_cols] = tap[main:, main:]


def pack_kernels(local_kernel, global_kernel):
    width = packed_width(local_kernel.shape[2])[2]
    shape = jax.ShapeDtypeStruct((width, width), BF16)
    return pl.pallas_call(
        pack_body,
        out_shape=(shape, shape),
        in_specs=[pl.BlockSpec(memory_space=pltpu.VMEM)] * 2,
        out_specs=(pl.BlockSpec(memory_space=pltpu.VMEM),) * 2,
        compiler_params=pltpu.CompilerParams(vmem_limit_bytes=24 << 20),
        cost_estimate=pl.CostEstimate(
            flops=0, bytes_accessed=8 * local_kernel.size, transcendentals=0
        ),
        name="pack_kernels",
    )(local_kernel, global_kernel)


def main_body(
    dil_rows,
    group_size,
    crop_count,
    image_count,
    table,
    x_ref,
    top_ref,
    bottom_ref,
    crop_ref,
    above_ref,
    below_ref,
    image_ref,
    affine_ref,
    local_w,
    global_w,
    out_ref,
    column_coef,
    local_x,
    global_x,
    local_p,
    global_p,
    out_buf,
    out_sem,
):
    rows, columns, channels = x_ref.shape
    main, left, width = packed_width(channels)
    crops = columns // CROP
    split_row = table[0]
    split_col = table[1]
    image_col = table[2]
    local_valid = [table[8 + i] != 0 for i in range(rows + 1)]
    global_valid = [table[8 + rows + 1 + i] != 0 for i in range(rows + dil_rows)]

    lane = lax.broadcasted_iota(jnp.int32, (8, LANES), 1)
    crop_tile = crop_ref[...] + jnp.where(
        lane < 64, pltpu.roll(above_ref[...], 64, 1), pltpu.roll(below_ref[...], 64, 1)
    )
    tiles = [(crop_tile, crop_count)]
    for t in range(image_ref.shape[1] // LANES):
        tiles.append((image_ref[:, t * LANES : (t + 1) * LANES], image_count))
    stack = []
    for tile, count in tiles:
        mean = tile / count
        square = pltpu.roll(tile, 96, 1) / count
        inverse = lax.rsqrt(jnp.maximum(square - mean * mean, 0.0) + EPSILON)
        stack.append(jnp.where((lane & 63) < 32, mean, 0.0))
        stack.append(jnp.where((lane & 63) < 32, inverse, 0.0))
    stack = jnp.concatenate(stack, axis=0)
    slots = [
        exact_dot(stack, selector_matrix((LANES, channels), 1, group_size, offset))
        for offset in (0, 64)
    ]

    def coefficients(tile, slot, row):
        mean = slots[slot][16 * tile : 16 * tile + 8]
        inverse = slots[slot][16 * tile + 8 : 16 * tile + 16]
        scale = inverse * affine_ref[row : row + 1, :] * 0.5
        shift = affine_ref[row + 1 : row + 2, :] * 0.5 - mean * scale
        return scale, shift

    for slot in range(2):
        pair = coefficients(0, slot, 0)
        for kind in range(2):
            for w in range(crops):
                own = pair[kind][w : w + 1, :]
                before = pair[kind][(w - 1) % crops : (w - 1) % crops + 1, :]
                col = lax.broadcasted_iota(jnp.int32, (CROP, channels), 0)
                column_coef[slot, kind, w * CROP : (w + 1) * CROP, :] = jnp.where(
                    col >= split_col, own, before
                )
    image_coef = [coefficients(1 + p // 2, p % 2, 3) for p in range(dil_rows)]

    used = 3 * (main + left)

    def place(target, row, tap, act):
        base = row * columns
        span = slice(base, base + columns)
        target[span, tap * main : tap * main + main] = act[:, :main]
        if left:
            low = 3 * main + tap * left
            target[span, low : low + left] = act[:, main:]

    def spread(target, row, step, act, valid_before, valid_after):
        zero = jnp.zeros_like(act)
        if 0 <= row < rows:
            place(target, row, 1, act)
        if 0 <= row + step < rows:
            place(target, row + step, 0, jnp.where(valid_after, act, zero))
        if 0 <= row - step < rows:
            place(target, row - step, 2, jnp.where(valid_before, act, zero))

    def source(row):
        if row < 0:
            return top_ref[dil_rows + row]
        if row >= rows:
            return bottom_ref[row - rows]
        return x_ref[row]

    def activation(half):
        return (half + half * jnp.tanh(half)).astype(BF16)

    def local_row(row):
        slot = jnp.where(min(max(row, 0), rows - 1) < split_row, 0, 1)
        half = source(row).astype(F32) * column_coef[slot, 0] + column_coef[slot, 1]
        before = local_valid[row] if row >= 0 else None
        after = local_valid[row + 1] if row < rows else None
        spread(local_x, row, 1, activation(half), before, after)

    def global_row(row):
        scale, shift = image_coef[row % dil_rows]
        value = source(row).astype(F32).reshape(columns // 8, 8, channels)
        half = (value * scale[None] + shift[None]).reshape(columns, channels)
        before = global_valid[row] if row >= 0 else None
        after = global_valid[row + dil_rows] if row < rows else None
        spread(global_x, row, dil_rows, activation(half), before, after)

    if used < width:
        for target in (local_x, global_x):
            target[:, width - LANES :] = jnp.zeros((rows * columns, LANES), BF16)

    col8 = lax.broadcasted_iota(jnp.int32, (columns, LANES), 0)
    image_q = (col8 // 8 - image_col) & (columns // 8 - 1)
    image_left = image_q != 0
    image_right = image_q != columns // 8 - 1
    crop_c = (col8 - split_col) & (CROP - 1)
    crop_left = crop_c != 0
    crop_right = crop_c != CROP - 1

    def piece(ref, base, tap, start, size):
        span = slice(base, base + columns)
        if start < main:
            return ref[span, tap * main + start : tap * main + start + size]
        low = 3 * main + tap * left
        return ref[span, low : low + size]

    def combine(ref, base, step, mask_left, mask_right, start, size):
        centre = piece(ref, base, 1, start, size)
        from_left = pltpu.roll(piece(ref, base, 0, start, size), step, 0)
        from_right = pltpu.roll(piece(ref, base, 2, start, size), columns - step, 0)
        centre = centre + jnp.where(mask_left[:, :size], from_left, 0.0)
        return centre + jnp.where(mask_right[:, :size], from_right, 0.0)

    pair_rows = 2
    done_local = -1
    done_global = -dil_rows
    copies = []
    for pair in range(rows // pair_rows):
        last = pair * pair_rows + pair_rows - 1
        span = slice(pair * pair_rows * columns, (pair + 1) * pair_rows * columns)
        while done_local <= last + 1:
            local_row(done_local)
            done_local += 1
        local_p[...] = jnp.dot(local_x[span, :], local_w[...], preferred_element_type=F32)
        while done_global <= last + dil_rows:
            global_row(done_global)
            done_global += 1
        global_p[...] = jnp.dot(global_x[span, :], global_w[...], preferred_element_type=F32)
        for r in range(pair_rows):
            row = pair * pair_rows + r
            for start in range(0, channels, LANES):
                size = min(LANES, channels - start)
                lanes = slice(start, start + size)
                local_sum = combine(local_p, r * columns, 1, crop_left, crop_right, start, size)
                global_sum = combine(global_p, r * columns, 8, image_left, image_right, start, size)
                local_sum = local_sum + affine_ref[2:3, lanes]
                global_sum = (global_sum + affine_ref[5:6, lanes]).astype(BF16)
                out_buf[row, :, lanes] = (local_sum + global_sum.astype(F32)).astype(BF16)
        window = pl.ds(pair * pair_rows, pair_rows)
        copy = pltpu.make_async_copy(out_buf.at[window], out_ref.at[window], out_sem.at[pair])
        copy.start()
        copies.append(copy)
    for copy in copies:
        copy.wait()


def main_call(latent, top, bottom, crop, above, below, image, affine, local_w, global_w, table):
    rows, columns, channels = latent.shape
    dil_rows = top.shape[0]
    width = local_w.shape[0]
    vmem = pl.BlockSpec(memory_space=pltpu.VMEM)
    group_size = channels // NORM_GROUPS
    image_count = (rows * lax.axis_size("rows") // dil_rows) * (columns // DILATION_COLUMNS)
    return pl.pallas_call(
        functools.partial(
            main_body,
            dil_rows,
            group_size,
            float(CROP * CROP * group_size),
            float(image_count * group_size),
        ),
        out_shape=jax.ShapeDtypeStruct(latent.shape, BF16),
        in_specs=[pl.BlockSpec(memory_space=pltpu.SMEM)] + [vmem] * 10,
        out_specs=pl.BlockSpec(memory_space=pl.ANY),
        scratch_shapes=[
            pltpu.VMEM((2, 2, columns, channels), F32),
            pltpu.VMEM((rows * columns, width), BF16),
            pltpu.VMEM((rows * columns, width), BF16),
            pltpu.VMEM((2 * columns, width), F32),
            pltpu.VMEM((2 * columns, width), F32),
            pltpu.VMEM(latent.shape, BF16),
            pltpu.SemaphoreType.DMA((rows // 2,)),
        ],
        compiler_params=pltpu.CompilerParams(vmem_limit_bytes=44 << 20),
        cost_estimate=pl.CostEstimate(
            flops=4 * rows * columns * width * width,
            bytes_accessed=4 * latent.size,
            transcendentals=2 * latent.size,
        ),
        name="crop_and_dilated",
    )(table, latent, top, bottom, crop, above, below, image, affine, local_w, global_w)


def shards(
    latent,
    crop_shift,
    dilation_shift,
    local_gain,
    local_bias,
    local_kernel,
    local_offset,
    global_gain,
    global_bias,
    global_kernel,
    global_offset,
):
    rows, columns, channels = latent.shape
    devices = lax.axis_size("rows")
    dil_rows = devices // DILATION_COLUMNS
    sub_rows = rows * devices // dil_rows
    sub_cols = columns // DILATION_COLUMNS
    first = lax.axis_index("rows") * rows

    def shifted(value, step):
        return lax.ppermute(value, "rows", [(i, (i + step) % devices) for i in range(devices)])

    def exchanged(value, bit):
        return lax.ppermute(value, "rows", [(i, i ^ bit) for i in range(devices)])

    top = shifted(latent[rows - dil_rows :], 1)
    bottom = shifted(latent[:dil_rows], -1)

    split_row = jnp.clip(jnp.mod(crop_shift[0], CROP) - jnp.mod(first, CROP), 0, rows)
    split_col = jnp.mod(crop_shift[1], CROP)
    image_row = jnp.mod(dilation_shift[0], sub_rows)
    image_col = jnp.mod(dilation_shift[1], sub_cols)
    edges = first + jnp.arange(rows + 1, dtype=jnp.int32)
    local_ok = (jnp.mod(edges - crop_shift[0], CROP) != 0).astype(jnp.int32)
    edges = first + jnp.arange(rows + dil_rows, dtype=jnp.int32)
    global_ok = (jnp.mod(edges // dil_rows - image_row, sub_rows) != 0).astype(jnp.int32)
    head = jnp.stack([split_row, split_col, image_col] + [jnp.zeros((), jnp.int32)] * 5)
    table = jnp.concatenate([head, local_ok, global_ok]).astype(jnp.int32)

    totals = strip_statistics(latent, table, dil_rows)
    local_w, global_w = pack_kernels(local_kernel, global_kernel)

    span = CROP // rows
    bit = 1
    while bit < span:
        totals = totals + exchanged(totals, bit)
        bit *= 2
    above = shifted(totals, span)
    below = shifted(totals, -span)
    image = totals[:, LANES:]
    if devices == 4 * span:
        image = (image + above[:, LANES:]) + (below[:, LANES:] + shifted(image, 2 * span))
    else:
        while bit < devices:
            image = image + exchanged(image, bit)
            bit *= 2
    affine = jnp.stack(
        [local_gain, local_bias, local_offset, global_gain, global_bias, global_offset]
    )
    return main_call(
        latent,
        top,
        bottom,
        totals[:, :LANES],
        above[:, :LANES],
        below[:, :LANES],
        image,
        affine,
        local_w,
        global_w,
        table,
    )


def solution(mesh):
    return jax.shard_map(
        shards,
        mesh=mesh,
        in_specs=(
            P(("groups", "rows"), None, None),
            P("groups"),
            P("groups"),
            P(),
            P(),
            P(),
            P(),
            P(),
            P(),
            P(),
            P(),
        ),
        out_specs=P(("groups", "rows"), None, None),
        check_vma=False,
    )
```

```python
import functools

import jax
import jax.numpy as jnp
from jax import lax
from jax.experimental import pallas as pl
from jax.experimental.pallas import tpu as pltpu
from jax.sharding import PartitionSpec as P

NORM_GROUPS = 32
DILATION_COLUMNS = 8
CROP = 32
EPSILON = 1e-05
LANES = 128

BF16 = jnp.bfloat16
F32 = jnp.float32


def split3(value):
    high = value.astype(BF16)
    rest = value - high.astype(F32)
    middle = rest.astype(BF16)
    low = (rest - middle.astype(F32)).astype(BF16)
    return high, middle, low


def one_hot(condition):
    return jnp.where(condition, 1.0, 0.0).astype(BF16)


def group_selector(shape, channel_dim, group_size):
    channel = lax.broadcasted_iota(jnp.int32, shape, channel_dim)
    first = (lax.broadcasted_iota(jnp.int32, shape, 1 - channel_dim) & 31) * group_size
    return one_hot((channel >= first) & (channel < first + group_size))


def lane_plan(columns, dil_rows):
    crops = columns // CROP
    used = 2 * crops + DILATION_COLUMNS * dil_rows
    return crops, used, -(-2 * used // LANES) * LANES


def crop_of(column, split_col, columns):
    return ((column - split_col) & (columns - 1)) // CROP


def split_of_strip(crop_shift, rows):
    first = lax.axis_index("rows") * rows
    return jnp.clip(jnp.remainder(crop_shift, CROP) - jnp.remainder(first, CROP), 0, rows)


def stats_body(dil_rows, group_size, crop_shift, x_hbm, out_ref, x_buf, selectors, sems):
    rows, channels, columns = x_buf.shape
    crops, used, width = lane_plan(columns, dil_rows)
    copies = []
    for r in range(rows):
        copy = pltpu.make_async_copy(x_hbm.at[r], x_buf.at[r], sems.at[r])
        copy.start()
        copies.append(copy)
    split_row = split_of_strip(crop_shift[0], rows)
    split_col = jnp.remainder(crop_shift[1], CROP)
    column = lax.broadcasted_iota(jnp.int32, (columns, width), 0)
    lane = lax.broadcasted_iota(jnp.int32, (columns, width), 1)
    crop_lane = lane - crop_of(column, split_col, columns)
    image_lane = lane - 2 * crops - (column & (DILATION_COLUMNS - 1))
    for slot in range(2):
        for p in range(dil_rows):
            for k in range(2):
                at_crop = crop_lane == slot * crops + k * used
                at_image = image_lane == p * DILATION_COLUMNS + k * used
                selectors[slot, p, k * columns : (k + 1) * columns] = one_hot(at_crop | at_image)
    total = None
    for r in range(rows):
        copies[r].wait()
        value = x_buf[r]
        wide = value.astype(F32)
        square = wide * wide
        high = square.astype(BF16)
        low = (square - high.astype(F32)).astype(BF16)
        slot = jnp.where(r < split_row, 0, 1)
        plain = selectors[slot, r % dil_rows, :columns]
        squares = selectors[slot, r % dil_rows, columns:]
        part = jnp.dot(
            jnp.concatenate([value, high, low], axis=1),
            jnp.concatenate([plain, squares, squares], axis=0),
            preferred_element_type=F32,
        )
        total = part if total is None else total + part
    groups = group_selector((NORM_GROUPS, channels), 1, group_size)
    high, middle, low = split3(total)
    parts = [jnp.dot(groups, part, preferred_element_type=F32) for part in (low, middle, high)]
    out_ref[...] = (parts[0] + parts[1]) + parts[2]


def strip_statistics(strip, crop_shift, dil_rows):
    rows, channels, columns = strip.shape
    crops, used, width = lane_plan(columns, dil_rows)
    return pl.pallas_call(
        functools.partial(stats_body, dil_rows, channels // NORM_GROUPS),
        out_shape=jax.ShapeDtypeStruct((NORM_GROUPS, width), F32),
        in_specs=[
            pl.BlockSpec(memory_space=pltpu.SMEM),
            pl.BlockSpec(memory_space=pl.ANY),
        ],
        out_specs=pl.BlockSpec(memory_space=pltpu.VMEM),
        scratch_shapes=[
            pltpu.VMEM(strip.shape, BF16),
            pltpu.VMEM((2, dil_rows, 2 * columns, width), BF16),
            pltpu.SemaphoreType.DMA((rows,)),
        ],
        compiler_params=pltpu.CompilerParams(vmem_limit_bytes=16 << 20),
        cost_estimate=pl.CostEstimate(
            flops=12 * strip.size, bytes_accessed=2 * strip.size, transcendentals=0
        ),
        name="strip_statistics",
    )(crop_shift, strip)


def pack_body(local_ref, global_ref, affine_ref, weight_out, affine_out):
    taps, channels = local_ref.shape[0] * local_ref.shape[1], local_ref.shape[2]
    local_rows = [local_ref[t // 3, t % 3] for t in range(taps)]
    global_rows = [global_ref[t // 3, t % 3] for t in range(taps)]
    stacked = jnp.concatenate(local_rows + global_rows, axis=0)
    for start in range(0, 2 * taps * channels, LANES):
        weight_out[:, start : start + LANES] = stacked[start : start + LANES].T
    count = affine_ref.shape[0]
    padded = jnp.concatenate([affine_ref[...], jnp.zeros((LANES - count, channels), F32)], axis=0)
    affine_out[...] = padded.T


def pack_parameters(local_kernel, global_kernel, affine):
    channels = local_kernel.shape[2]
    vmem = pl.BlockSpec(memory_space=pltpu.VMEM)
    return pl.pallas_call(
        pack_body,
        out_shape=(
            jax.ShapeDtypeStruct((channels, 18 * channels), BF16),
            jax.ShapeDtypeStruct((channels, LANES), F32),
        ),
        in_specs=[vmem] * 3,
        out_specs=(vmem, vmem),
        compiler_params=pltpu.CompilerParams(vmem_limit_bytes=16 << 20),
        cost_estimate=pl.CostEstimate(
            flops=0, bytes_accessed=8 * local_kernel.size, transcendentals=0
        ),
        name="pack_parameters",
    )(local_kernel, global_kernel, affine)


def main_body(
    dil_rows,
    group_size,
    image_cells,
    crop_shift,
    dilation_shift,
    x_ref,
    top_ref,
    bottom_ref,
    own_ref,
    above_ref,
    below_ref,
    image_ref,
    affine_ref,
    weight_ref,
    out_ref,
    crop_coef,
    image_coef,
    local_act,
    global_act,
    out_buf,
    out_sem,
):
    rows, channels, columns = x_ref.shape
    crops, used, width = lane_plan(columns, dil_rows)
    sub_cols = columns // DILATION_COLUMNS
    first = lax.axis_index("rows") * rows
    sub_rows = image_cells // sub_cols
    split_row = split_of_strip(crop_shift[0], rows)
    split_col = jnp.remainder(crop_shift[1], CROP)
    image_row = jnp.remainder(dilation_shift[0], sub_rows)
    image_col = jnp.remainder(dilation_shift[1], sub_cols)

    def local_valid(row):
        return jnp.remainder(first + row - jnp.remainder(crop_shift[0], CROP) + CROP, CROP) != 0

    def global_valid(row):
        place = lax.div(first + row, dil_rows) - image_row + sub_rows
        return jnp.remainder(place, sub_rows) != 0

    lane = lax.broadcasted_iota(jnp.int32, (NORM_GROUPS, width), 1)
    inner = jnp.where(lane < used, lane, lane - used)
    own = own_ref[...]
    neighbour = jnp.where(
        inner < crops,
        pltpu.roll(above_ref[...], width - crops, 1),
        pltpu.roll(below_ref[...], crops, 1),
    )
    total = jnp.where(inner < 2 * crops, own + neighbour, image_ref[...])
    count = jnp.where(inner < 2 * crops, CROP * CROP * group_size, image_cells * group_size)
    average = total / count.astype(F32)
    square = pltpu.roll(average, width - used, 1)
    inverse = lax.rsqrt(jnp.maximum(square - average * average, 0.0) + EPSILON)
    moments = jnp.where(lane < used, average, pltpu.roll(inverse, used, 1))
    moments = jnp.where(lane < 2 * used, moments, 0.0)
    groups = group_selector((channels, 3 * NORM_GROUPS), 0, group_size)
    spread = jnp.dot(
        groups, jnp.concatenate(split3(moments), axis=0), preferred_element_type=F32
    )
    lane = lax.broadcasted_iota(jnp.int32, (channels, width), 1)
    at_crop = lane < 2 * crops
    gain = jnp.where(at_crop, affine_ref[:, 0:1], affine_ref[:, 2:3]) * 0.5
    bias = jnp.where(at_crop, affine_ref[:, 1:2], affine_ref[:, 3:4]) * 0.5
    scale = pltpu.roll(spread, width - used, 1) * gain
    shift = bias - spread * scale
    pieces = []
    for value in (scale, shift):
        pieces.extend(split3(jnp.where(lane < used, value, 0.0)))
    selector_lane = lax.broadcasted_iota(jnp.int32, (width, columns), 0)
    column = lax.broadcasted_iota(jnp.int32, (width, columns), 1)
    crop = crop_of(column, split_col, columns)
    for slot in range(2):
        chosen = one_hot(selector_lane == crop + slot * crops)
        for k in range(2):
            parts = [jnp.dot(piece, chosen, preferred_element_type=F32) for piece in pieces[3 * k : 3 * k + 3]]
            crop_coef[slot, k] = (parts[2] + parts[1]) + parts[0]
    for p in range(dil_rows):
        phase = column[:, :LANES] & (DILATION_COLUMNS - 1)
        chosen = one_hot(selector_lane[:, :LANES] == phase + 2 * crops + p * DILATION_COLUMNS)
        for k in range(2):
            parts = [jnp.dot(piece, chosen, preferred_element_type=F32) for piece in pieces[3 * k : 3 * k + 3]]
            image_coef[p, k] = (parts[2] + parts[1]) + parts[0]

    column = lax.broadcasted_iota(jnp.int32, (16, columns), 1)
    crop_col = (column - split_col) & (CROP - 1)
    image_q = (lax.shift_right_logical(column, 3) - image_col) & (sub_cols - 1)
    crop_left = one_hot(crop_col != 0)[:1]
    crop_right = one_hot(crop_col != CROP - 1)[:1]
    image_left = one_hot(image_q != 0)[:1]
    image_right = one_hot(image_q != sub_cols - 1)[:1]

    def source(row):
        if row < 0:
            return top_ref[dil_rows + row].astype(F32)
        if row >= rows:
            return bottom_ref[row - rows].astype(F32)
        return x_ref[row].astype(F32)

    def store(target, half, step, mask_left, mask_right):
        act = (half + half * jnp.tanh(half)).astype(BF16)
        target[0:channels] = pltpu.roll(act, step, 1) * mask_left
        target[channels : 2 * channels] = act
        target[2 * channels :] = pltpu.roll(act, columns - step, 1) * mask_right

    def local_row(row):
        slot = jnp.where(min(max(row, 0), rows - 1) < split_row, 0, 1)
        half = source(row) * crop_coef[slot, 0] + crop_coef[slot, 1]
        store(local_act.at[row + 1], half, 1, crop_left, crop_right)

    def global_row(row):
        scale, shift = image_coef[row % dil_rows, 0], image_coef[row % dil_rows, 1]
        value = source(row)
        half = jnp.concatenate(
            [
                value[:, start : start + LANES] * scale + shift
                for start in range(0, columns, LANES)
            ],
            axis=1,
        )
        store(global_act.at[row + dil_rows], half, DILATION_COLUMNS, image_left, image_right)

    def taps(target, row, step, valid):
        zero = jnp.zeros((3 * channels, columns), BF16)
        return [
            jnp.where(valid(row), target[row], zero),
            target[row + step],
            jnp.where(valid(row + step), target[row + 2 * step], zero),
        ]

    offset = affine_ref[:, 4:5]
    done_local = -1
    done_global = -dil_rows
    copies = []
    for row in range(rows):
        while done_local <= row + 1:
            local_row(done_local)
            done_local += 1
        while done_global <= row + dil_rows:
            global_row(done_global)
            done_global += 1
        operand = jnp.concatenate(
            taps(local_act, row, 1, local_valid) + taps(global_act, row, dil_rows, global_valid),
            axis=0,
        )
        result = jnp.dot(weight_ref[...], operand, preferred_element_type=F32)
        out_buf[row] = (result + offset).astype(BF16)
        copy = pltpu.make_async_copy(out_buf.at[row], out_ref.at[row], out_sem.at[row])
        copy.start()
        copies.append(copy)
    for copy in copies:
        copy.wait()


def main_call(
    strip, top, bottom, own, above, below, image, affine, weights, crop_shift, dilation_shift
):
    rows, channels, columns = strip.shape
    dil_rows = top.shape[0]
    smem = pl.BlockSpec(memory_space=pltpu.SMEM)
    vmem = pl.BlockSpec(memory_space=pltpu.VMEM)
    image_cells = (rows * lax.axis_size("rows") // dil_rows) * (columns // DILATION_COLUMNS)
    return pl.pallas_call(
        functools.partial(main_body, dil_rows, channels // NORM_GROUPS, image_cells),
        out_shape=jax.ShapeDtypeStruct(strip.shape, BF16),
        in_specs=[smem, smem] + [vmem] * 9,
        out_specs=pl.BlockSpec(memory_space=pl.ANY),
        scratch_shapes=[
            pltpu.VMEM((2, 2, channels, columns), F32),
            pltpu.VMEM((dil_rows, 2, channels, LANES), F32),
            pltpu.VMEM((rows + 2, 3 * channels, columns), BF16),
            pltpu.VMEM((rows + 2 * dil_rows, 3 * channels, columns), BF16),
            pltpu.VMEM(strip.shape, BF16),
            pltpu.SemaphoreType.DMA((rows,)),
        ],
        compiler_params=pltpu.CompilerParams(vmem_limit_bytes=32 << 20),
        cost_estimate=pl.CostEstimate(
            flops=36 * channels * strip.size,
            bytes_accessed=4 * strip.size,
            transcendentals=2 * strip.size,
        ),
        name="crop_and_dilated",
    )(crop_shift, dilation_shift, strip, top, bottom, own, above, below, image, affine, weights)


def shards(
    latent,
    crop_shift,
    dilation_shift,
    local_gain,
    local_bias,
    local_kernel,
    local_offset,
    global_gain,
    global_bias,
    global_kernel,
    global_offset,
):
    rows, columns, channels = latent.shape
    devices = lax.axis_size("rows")
    dil_rows = devices // DILATION_COLUMNS
    strip = latent.transpose(0, 2, 1)

    def shifted(value, step):
        return lax.ppermute(value, "rows", [(i, (i + step) % devices) for i in range(devices)])

    def exchanged(value, bit):
        return lax.ppermute(value, "rows", [(i, i ^ bit) for i in range(devices)])

    top = shifted(strip[rows - dil_rows :], 1)
    bottom = shifted(strip[:dil_rows], -1)
    totals = strip_statistics(strip, crop_shift, dil_rows)
    affine = jnp.stack(
        [local_gain, local_bias, global_gain, global_bias, local_offset + global_offset]
        + [jnp.zeros_like(local_gain)] * 3
    )
    weights, affine = pack_parameters(local_kernel, global_kernel, affine)

    span = CROP // rows
    bit = 1
    while bit < span:
        totals = totals + exchanged(totals, bit)
        bit *= 2
    above = shifted(totals, span)
    below = shifted(totals, -span)
    if devices == 4 * span:
        image = (totals + above) + (below + shifted(totals, 2 * span))
    else:
        image = totals
        while bit < devices:
            image = image + exchanged(image, bit)
            bit *= 2
    result = main_call(
        strip, top, bottom, totals, above, below, image, affine, weights, crop_shift, dilation_shift
    )
    return result.transpose(0, 2, 1)


def solution(mesh):
    return jax.shard_map(
        shards,
        mesh=mesh,
        in_specs=(
            P(("groups", "rows"), None, None),
            P("groups"),
            P("groups"),
            P(),
            P(),
            P(),
            P(),
            P(),
            P(),
            P(),
            P(),
        ),
        out_specs=P(("groups", "rows"), None, None),
        check_vma=False,
    )
```

```python
import functools

import jax
import jax.numpy as jnp
from jax import lax
from jax.experimental import pallas as pl
from jax.experimental.pallas import tpu as pltpu
from jax.sharding import PartitionSpec as P

NORM_GROUPS = 32
DILATION_COLUMNS = 8
CROP = 32
EPSILON = 1e-05
LANES = 128

BF16 = jnp.bfloat16
F32 = jnp.float32


def split3(value):
    high = value.astype(BF16)
    rest = value - high.astype(F32)
    middle = rest.astype(BF16)
    low = (rest - middle.astype(F32)).astype(BF16)
    return high, middle, low


def in_hbm(value):
    return pltpu.with_memory_space_constraint(value, pltpu.HBM)


def one_hot(condition):
    return jnp.where(condition, 1.0, 0.0).astype(BF16)


def group_selector(shape, channel_dim, group_size):
    channel = lax.broadcasted_iota(jnp.int32, shape, channel_dim)
    first = (lax.broadcasted_iota(jnp.int32, shape, 1 - channel_dim) & 31) * group_size
    return one_hot((channel >= first) & (channel < first + group_size))


def lane_plan(columns, dil_rows):
    crops = columns // CROP
    used = 2 * crops + DILATION_COLUMNS * dil_rows
    return crops, used, -(-2 * used // LANES) * LANES


def crop_of(column, split_col, columns):
    return ((column - split_col) & (columns - 1)) // CROP


def split_of_strip(crop_shift, rows):
    first = lax.axis_index("rows") * rows
    return jnp.clip(jnp.remainder(crop_shift, CROP) - jnp.remainder(first, CROP), 0, rows)


def stats_body(
    dil_rows,
    group_size,
    shift_hbm,
    x_hbm,
    local_hbm,
    global_hbm,
    out_ref,
    pair_ref,
    other_ref,
    local_out,
    global_out,
    x_buf,
    crop_shift,
    selectors,
    shift_sem,
    sems,
):
    rows, channels, columns = x_buf.shape
    crops, used, width = lane_plan(columns, dil_rows)
    shift_copy = pltpu.make_async_copy(shift_hbm, crop_shift, shift_sem)
    shift_copy.start()
    copy = pltpu.make_async_copy(x_hbm, x_buf, sems.at[0])
    copy.start()
    later = [
        pltpu.make_async_copy(local_hbm, local_out, sems.at[1]),
        pltpu.make_async_copy(global_hbm, global_out, sems.at[2]),
    ]
    for kernel_copy in later:
        kernel_copy.start()
    shift_copy.wait()
    split_row = split_of_strip(crop_shift[0], rows)
    split_col = jnp.remainder(crop_shift[1], CROP)
    column = lax.broadcasted_iota(jnp.int32, (columns, width), 0)
    lane = lax.broadcasted_iota(jnp.int32, (columns, width), 1)
    crop_lane = lane - crop_of(column, split_col, columns)
    image_lane = lane - 2 * crops - (column & (DILATION_COLUMNS - 1))
    for slot in range(2):
        for p in range(dil_rows):
            for k in range(2):
                at_crop = crop_lane == slot * crops + k * used
                at_image = image_lane == p * DILATION_COLUMNS + k * used
                selectors[slot, p, k * columns : (k + 1) * columns] = one_hot(at_crop | at_image)
    groups = group_selector((NORM_GROUPS, channels), 1, group_size)
    copy.wait()
    odd = lax.axis_index("rows") & 1
    pair_ref[...] = x_buf[pl.ds(jnp.where(odd == 1, 0, rows - dil_rows), dil_rows)]
    other_ref[...] = x_buf[pl.ds(jnp.where(odd == 1, rows - dil_rows, 0), dil_rows)]
    total = None
    for r in range(rows):
        value = x_buf[r]
        wide = value.astype(F32)
        square = wide * wide
        high = square.astype(BF16)
        low = (square - high.astype(F32)).astype(BF16)
        slot = jnp.where(r < split_row, 0, 1)
        plain = selectors[slot, r % dil_rows, :columns]
        squares = selectors[slot, r % dil_rows, columns:]
        part = jnp.dot(
            jnp.concatenate([value, high, low], axis=1),
            jnp.concatenate([plain, squares, squares], axis=0),
            preferred_element_type=F32,
        )
        total = part if total is None else total + part
    high, middle, low = split3(total)
    parts = [jnp.dot(groups, part, preferred_element_type=F32) for part in (low, middle, high)]
    out_ref[...] = (parts[0] + parts[1]) + parts[2]
    for kernel_copy in later:
        kernel_copy.wait()


def strip_statistics(strip, crop_shift, local_kernel, global_kernel, dil_rows):
    rows, channels, columns = strip.shape
    crops, used, width = lane_plan(columns, dil_rows)
    edge = jax.ShapeDtypeStruct((dil_rows, channels, columns), BF16)
    kernel = jax.ShapeDtypeStruct(local_kernel.shape, BF16)
    vmem = pl.BlockSpec(memory_space=pltpu.VMEM)
    return pl.pallas_call(
        functools.partial(stats_body, dil_rows, channels // NORM_GROUPS),
        out_shape=(
            jax.ShapeDtypeStruct((NORM_GROUPS, width), F32),
            edge,
            edge,
            kernel,
            kernel,
            jax.ShapeDtypeStruct(strip.shape, BF16),
        ),
        in_specs=[pl.BlockSpec(memory_space=pltpu.HBM)] * 4,
        out_specs=(vmem,) * 6,
        scratch_shapes=[
            pltpu.SMEM(crop_shift.shape, jnp.int32),
            pltpu.VMEM((2, dil_rows, 2 * columns, width), BF16),
            pltpu.SemaphoreType.DMA(()),
            pltpu.SemaphoreType.DMA((3,)),
        ],
        compiler_params=pltpu.CompilerParams(vmem_limit_bytes=16 << 20),
        cost_estimate=pl.CostEstimate(
            flops=12 * strip.size, bytes_accessed=2 * strip.size, transcendentals=0
        ),
        name="strip_statistics",
    )(in_hbm(crop_shift), in_hbm(strip), in_hbm(local_kernel), in_hbm(global_kernel))


def pack_body(local_ref, global_ref, *refs):
    vectors, (weight_out, affine_out, rows, sems) = refs[:-4], refs[-4:]
    channels = local_ref.shape[2]
    copies = []
    for i, vector in enumerate(vectors):
        copy = pltpu.make_async_copy(vector, rows.at[i], sems.at[i])
        copy.start()
        copies.append(copy)
    taps = [ref[t // 3, t % 3] for ref in (local_ref, global_ref) for t in range(9)]
    stacked = jnp.concatenate(taps, axis=0)
    for start in range(0, stacked.shape[0], LANES):
        weight_out[:, start : start + LANES] = stacked[start : start + LANES].T
    for copy in copies:
        copy.wait()
    table = [rows[i].reshape(1, channels) for i in range(len(vectors))]
    table.append(jnp.zeros((LANES - len(vectors), channels), F32))
    affine_out[...] = jnp.concatenate(table, axis=0).T


def pack_parameters(local_kernel, global_kernel, vectors):
    channels = local_kernel.shape[2]
    vmem = pl.BlockSpec(memory_space=pltpu.VMEM)
    return pl.pallas_call(
        pack_body,
        out_shape=(
            jax.ShapeDtypeStruct((channels, 18 * channels), BF16),
            jax.ShapeDtypeStruct((channels, LANES), F32),
        ),
        in_specs=[vmem] * 2 + [pl.BlockSpec(memory_space=pltpu.HBM)] * len(vectors),
        out_specs=(vmem, vmem),
        scratch_shapes=[
            pltpu.VMEM((len(vectors), channels), F32),
            pltpu.SemaphoreType.DMA((len(vectors),)),
        ],
        compiler_params=pltpu.CompilerParams(vmem_limit_bytes=12 << 20),
        cost_estimate=pl.CostEstimate(
            flops=0, bytes_accessed=8 * local_kernel.size, transcendentals=0
        ),
        name="pack_parameters",
    )(local_kernel, global_kernel, *[in_hbm(vector) for vector in vectors])


def main_body(
    dil_rows,
    group_size,
    image_cells,
    crop_shift,
    dilation_shift,
    x_ref,
    pair_ref,
    other_ref,
    own_ref,
    above_ref,
    below_ref,
    image_ref,
    affine_ref,
    weight_ref,
    out_ref,
    crop_coef,
    image_coef,
    local_act,
    global_act,
    out_buf,
    out_sem,
):
    rows, channels, columns = x_ref.shape
    crops, used, width = lane_plan(columns, dil_rows)
    sub_cols = columns // DILATION_COLUMNS
    first = lax.axis_index("rows") * rows
    sub_rows = image_cells // sub_cols
    split_row = split_of_strip(crop_shift[0], rows)
    split_col = jnp.remainder(crop_shift[1], CROP)
    image_row = jnp.remainder(dilation_shift[0], sub_rows)
    image_col = jnp.remainder(dilation_shift[1], sub_cols)

    def local_valid(row):
        return jnp.remainder(first + row - jnp.remainder(crop_shift[0], CROP) + CROP, CROP) != 0

    def global_valid(row):
        place = lax.div(first + row, dil_rows) - image_row + sub_rows
        return jnp.remainder(place, sub_rows) != 0

    lane = lax.broadcasted_iota(jnp.int32, (NORM_GROUPS, width), 1)
    inner = jnp.where(lane < used, lane, lane - used)
    own = own_ref[...]
    neighbour = jnp.where(
        inner < crops,
        pltpu.roll(above_ref[...], width - crops, 1),
        pltpu.roll(below_ref[...], crops, 1),
    )
    total = jnp.where(inner < 2 * crops, own + neighbour, image_ref[...])
    count = jnp.where(inner < 2 * crops, CROP * CROP * group_size, image_cells * group_size)
    average = total / count.astype(F32)
    square = pltpu.roll(average, width - used, 1)
    inverse = lax.rsqrt(jnp.maximum(square - average * average, 0.0) + EPSILON)
    moments = jnp.where(lane < used, average, pltpu.roll(inverse, used, 1))
    moments = jnp.where(lane < 2 * used, moments, 0.0)
    groups = group_selector((channels, 3 * NORM_GROUPS), 0, group_size)
    spread = jnp.dot(
        groups, jnp.concatenate(split3(moments), axis=0), preferred_element_type=F32
    )
    lane = lax.broadcasted_iota(jnp.int32, (channels, width), 1)
    at_crop = lane < 2 * crops
    gain = jnp.where(at_crop, affine_ref[:, 0:1], affine_ref[:, 2:3]) * 0.5
    bias = jnp.where(at_crop, affine_ref[:, 1:2], affine_ref[:, 3:4]) * 0.5
    scale = pltpu.roll(spread, width - used, 1) * gain
    shift = bias - spread * scale
    pieces = []
    for value in (scale, shift):
        pieces.extend(split3(jnp.where(lane < used, value, 0.0)))
    selector_lane = lax.broadcasted_iota(jnp.int32, (width, columns), 0)
    column = lax.broadcasted_iota(jnp.int32, (width, columns), 1)
    crop = crop_of(column, split_col, columns)
    for slot in range(2):
        chosen = one_hot(selector_lane == crop + slot * crops)
        for k in range(2):
            parts = [jnp.dot(piece, chosen, preferred_element_type=F32) for piece in pieces[3 * k : 3 * k + 3]]
            crop_coef[slot, k] = (parts[2] + parts[1]) + parts[0]
    for p in range(dil_rows):
        phase = column[:, :LANES] & (DILATION_COLUMNS - 1)
        chosen = one_hot(selector_lane[:, :LANES] == phase + 2 * crops + p * DILATION_COLUMNS)
        for k in range(2):
            parts = [jnp.dot(piece, chosen, preferred_element_type=F32) for piece in pieces[3 * k : 3 * k + 3]]
            image_coef[p, k] = (parts[2] + parts[1]) + parts[0]

    column = lax.broadcasted_iota(jnp.int32, (16, columns), 1)
    crop_col = (column - split_col) & (CROP - 1)
    image_q = (lax.shift_right_logical(column, 3) - image_col) & (sub_cols - 1)
    crop_left = one_hot(crop_col != 0)[:1]
    crop_right = one_hot(crop_col != CROP - 1)[:1]
    image_left = one_hot(image_q != 0)[:1]
    image_right = one_hot(image_q != sub_cols - 1)[:1]

    odd = (lax.axis_index("rows") & 1) == 1

    def source(row):
        if row < 0:
            row += dil_rows
            return jnp.where(odd, pair_ref[row], other_ref[row]).astype(F32)
        if row >= rows:
            row -= rows
            return jnp.where(odd, other_ref[row], pair_ref[row]).astype(F32)
        return x_ref[row].astype(F32)

    def store(target, half, step, mask_left, mask_right):
        act = (half + half * jnp.tanh(half)).astype(BF16)
        target[0:channels] = pltpu.roll(act, step, 1) * mask_left
        target[channels : 2 * channels] = act
        target[2 * channels :] = pltpu.roll(act, columns - step, 1) * mask_right

    def local_row(row):
        slot = jnp.where(min(max(row, 0), rows - 1) < split_row, 0, 1)
        half = source(row) * crop_coef[slot, 0] + crop_coef[slot, 1]
        store(local_act.at[row + 1], half, 1, crop_left, crop_right)

    def global_row(row):
        scale, shift = image_coef[row % dil_rows, 0], image_coef[row % dil_rows, 1]
        value = source(row)
        half = jnp.concatenate(
            [
                value[:, start : start + LANES] * scale + shift
                for start in range(0, columns, LANES)
            ],
            axis=1,
        )
        store(global_act.at[row + dil_rows], half, DILATION_COLUMNS, image_left, image_right)

    def taps(target, row, step, valid):
        zero = jnp.zeros((3 * channels, columns), BF16)
        return [
            jnp.where(valid(row), target[row], zero),
            target[row + step],
            jnp.where(valid(row + step), target[row + 2 * step], zero),
        ]

    offset = affine_ref[:, 4:5] + affine_ref[:, 5:6]
    done_local = -1
    done_global = -dil_rows
    copies = []
    for row in range(rows):
        while done_local <= row + 1:
            local_row(done_local)
            done_local += 1
        while done_global <= row + dil_rows:
            global_row(done_global)
            done_global += 1
        operand = jnp.concatenate(
            taps(local_act, row, 1, local_valid) + taps(global_act, row, dil_rows, global_valid),
            axis=0,
        )
        result = jnp.dot(weight_ref[...], operand, preferred_element_type=F32)
        out_buf[row] = (result + offset).astype(BF16)
        copy = pltpu.make_async_copy(out_buf.at[row], out_ref.at[row], out_sem.at[row])
        copy.start()
        copies.append(copy)
    for copy in copies:
        copy.wait()


def main_call(
    strip, pair, other, own, above, below, image, affine, weights, crop_shift, dilation_shift
):
    rows, channels, columns = strip.shape
    dil_rows = pair.shape[0]
    smem = pl.BlockSpec(memory_space=pltpu.SMEM)
    vmem = pl.BlockSpec(memory_space=pltpu.VMEM)
    image_cells = (rows * lax.axis_size("rows") // dil_rows) * (columns // DILATION_COLUMNS)
    return pl.pallas_call(
        functools.partial(main_body, dil_rows, channels // NORM_GROUPS, image_cells),
        out_shape=jax.ShapeDtypeStruct(strip.shape, BF16),
        in_specs=[smem, smem] + [vmem] * 9,
        out_specs=pl.BlockSpec(memory_space=pl.ANY),
        scratch_shapes=[
            pltpu.VMEM((2, 2, channels, columns), F32),
            pltpu.VMEM((dil_rows, 2, channels, LANES), F32),
            pltpu.VMEM((rows + 2, 3 * channels, columns), BF16),
            pltpu.VMEM((rows + 2 * dil_rows, 3 * channels, columns), BF16),
            pltpu.VMEM(strip.shape, BF16),
            pltpu.SemaphoreType.DMA((rows,)),
        ],
        compiler_params=pltpu.CompilerParams(vmem_limit_bytes=32 << 20),
        cost_estimate=pl.CostEstimate(
            flops=36 * channels * strip.size,
            bytes_accessed=4 * strip.size,
            transcendentals=2 * strip.size,
        ),
        name="crop_and_dilated",
    )(crop_shift, dilation_shift, strip, pair, other, own, above, below, image, affine, weights)


def shards(
    latent,
    crop_shift,
    dilation_shift,
    local_gain,
    local_bias,
    local_kernel,
    local_offset,
    global_gain,
    global_bias,
    global_kernel,
    global_offset,
):
    rows, columns, channels = latent.shape
    devices = lax.axis_size("rows")
    dil_rows = devices // DILATION_COLUMNS
    strip = latent.transpose(0, 2, 1)

    def shifted(value, step):
        return lax.ppermute(value, "rows", [(i, (i + step) % devices) for i in range(devices)])

    def exchanged(value, bit):
        return lax.ppermute(value, "rows", [(i, i ^ bit) for i in range(devices)])

    def paired(value, start):
        links = [(i % devices, (i + 1) % devices) for i in range(start, devices + start, 2)]
        return lax.ppermute(value, "rows", links + [(b, a) for a, b in links])

    totals, pair, other, local_kernel, global_kernel, strip = strip_statistics(
        strip, crop_shift, local_kernel, global_kernel, dil_rows
    )
    span = CROP // rows
    bit = 1
    while bit < span:
        totals = totals + exchanged(totals, bit)
        if bit == 1:
            totals, pair, other, local_kernel = lax.optimization_barrier(
                (totals, pair, other, local_kernel)
            )
        bit *= 2
    vectors = (local_gain, local_bias, global_gain, global_bias, local_offset, global_offset)
    weights, affine = pack_parameters(local_kernel, global_kernel, vectors)
    totals, weights = lax.optimization_barrier((totals, weights))
    pair, other, weights = lax.optimization_barrier((pair, other, weights))
    pair = paired(pair, 0)
    other = paired(other, 1)
    above = shifted(totals, span)
    below = shifted(totals, -span)
    if devices == 4 * span:
        image = (totals + above) + (below + shifted(totals, 2 * span))
    else:
        image = totals
        while bit < devices:
            image = image + exchanged(image, bit)
            bit *= 2
    result = main_call(
        strip, pair, other, totals, above, below, image, affine, weights, crop_shift, dilation_shift
    )
    return result.transpose(0, 2, 1)


def solution(mesh):
    return jax.shard_map(
        shards,
        mesh=mesh,
        in_specs=(
            P(("groups", "rows"), None, None),
            P("groups"),
            P("groups"),
            P(),
            P(),
            P(),
            P(),
            P(),
            P(),
            P(),
            P(),
        ),
        out_specs=P(("groups", "rows"), None, None),
        check_vma=False,
    )
```

```python
import functools

import jax
import jax.numpy as jnp
from jax import lax
from jax.experimental import pallas as pl
from jax.experimental.pallas import tpu as pltpu
from jax.sharding import PartitionSpec as P

NORM_GROUPS = 32
DILATION_COLUMNS = 8
CROP = 32
EPSILON = 1e-05
LANES = 128

BF16 = jnp.bfloat16
F32 = jnp.float32


def split3(value):
    high = value.astype(BF16)
    rest = value - high.astype(F32)
    middle = rest.astype(BF16)
    low = (rest - middle.astype(F32)).astype(BF16)
    return high, middle, low


def in_hbm(value):
    return pltpu.with_memory_space_constraint(value, pltpu.HBM)


def one_hot(condition):
    return jnp.where(condition, 1.0, 0.0).astype(BF16)


def group_selector(shape, channel_dim, group_size):
    channel = lax.broadcasted_iota(jnp.int32, shape, channel_dim)
    first = (lax.broadcasted_iota(jnp.int32, shape, 1 - channel_dim) & 31) * group_size
    return one_hot((channel >= first) & (channel < first + group_size))


def lane_plan(columns, dil_rows):
    crops = columns // CROP
    used = 2 * crops + DILATION_COLUMNS * dil_rows
    return crops, used, -(-2 * used // LANES) * LANES


def crop_of(column, split_col, columns):
    return ((column - split_col) & (columns - 1)) // CROP


def split_of_strip(crop_shift, rows):
    first = lax.axis_index("rows") * rows
    return jnp.clip(jnp.remainder(crop_shift, CROP) - jnp.remainder(first, CROP), 0, rows)


def stats_body(
    dil_rows,
    group_size,
    shift_hbm,
    x_hbm,
    local_hbm,
    global_hbm,
    out_ref,
    pair_ref,
    other_ref,
    local_out,
    global_out,
    x_buf,
    crop_shift,
    selectors,
    shift_sem,
    sems,
):
    rows, channels, columns = x_buf.shape
    crops, used, width = lane_plan(columns, dil_rows)
    shift_copy = pltpu.make_async_copy(shift_hbm, crop_shift, shift_sem)
    shift_copy.start()
    copy = pltpu.make_async_copy(x_hbm, x_buf, sems.at[0])
    copy.start()
    later = [
        pltpu.make_async_copy(local_hbm, local_out, sems.at[1]),
        pltpu.make_async_copy(global_hbm, global_out, sems.at[2]),
    ]
    for kernel_copy in later:
        kernel_copy.start()
    shift_copy.wait()
    split_row = split_of_strip(crop_shift[0], rows)
    split_col = jnp.remainder(crop_shift[1], CROP)
    column = lax.broadcasted_iota(jnp.int32, (columns, width), 0)
    lane = lax.broadcasted_iota(jnp.int32, (columns, width), 1)
    crop_lane = lane - crop_of(column, split_col, columns)
    image_lane = lane - 2 * crops - (column & (DILATION_COLUMNS - 1))
    for slot in range(2):
        for p in range(dil_rows):
            for k in range(2):
                at_crop = crop_lane == slot * crops + k * used
                at_image = image_lane == p * DILATION_COLUMNS + k * used
                selectors[slot, p, k * columns : (k + 1) * columns] = one_hot(at_crop | at_image)
    groups = group_selector((NORM_GROUPS, channels), 1, group_size)
    copy.wait()
    odd = lax.axis_index("rows") & 1
    pair_ref[...] = x_buf[pl.ds(jnp.where(odd == 1, 0, rows - dil_rows), dil_rows)]
    other_ref[...] = x_buf[pl.ds(jnp.where(odd == 1, rows - dil_rows, 0), dil_rows)]
    total = None
    for r in range(rows):
        value = x_buf[r]
        wide = value.astype(F32)
        square = wide * wide
        high = square.astype(BF16)
        low = (square - high.astype(F32)).astype(BF16)
        slot = jnp.where(r < split_row, 0, 1)
        plain = selectors[slot, r % dil_rows, :columns]
        squares = selectors[slot, r % dil_rows, columns:]
        part = jnp.dot(
            jnp.concatenate([value, high, low], axis=1),
            jnp.concatenate([plain, squares, squares], axis=0),
            preferred_element_type=F32,
        )
        total = part if total is None else total + part
    high, middle, low = split3(total)
    parts = [jnp.dot(groups, part, preferred_element_type=F32) for part in (low, middle, high)]
    own = (parts[0] + parts[1]) + parts[2]
    lane = lax.broadcasted_iota(jnp.int32, (NORM_GROUPS, width), 1)
    inner = jnp.where(lane < used, lane, lane - used)
    upper = pltpu.roll(own, width - crops, 1)
    lower = pltpu.roll(own, crops, 1)
    out_ref[0] = own
    out_ref[1] = jnp.where(inner < crops, upper, jnp.where(inner < 2 * crops, lower, own))
    for kernel_copy in later:
        kernel_copy.wait()


def strip_statistics(strip, crop_shift, local_kernel, global_kernel, dil_rows):
    rows, channels, columns = strip.shape
    crops, used, width = lane_plan(columns, dil_rows)
    edge = jax.ShapeDtypeStruct((dil_rows, channels, columns), BF16)
    kernel = jax.ShapeDtypeStruct(local_kernel.shape, BF16)
    vmem = pl.BlockSpec(memory_space=pltpu.VMEM)
    return pl.pallas_call(
        functools.partial(stats_body, dil_rows, channels // NORM_GROUPS),
        out_shape=(
            jax.ShapeDtypeStruct((2, NORM_GROUPS, width), F32),
            edge,
            edge,
            kernel,
            kernel,
            jax.ShapeDtypeStruct(strip.shape, BF16),
        ),
        in_specs=[pl.BlockSpec(memory_space=pltpu.HBM)] * 4,
        out_specs=(vmem,) * 6,
        scratch_shapes=[
            pltpu.SMEM(crop_shift.shape, jnp.int32),
            pltpu.VMEM((2, dil_rows, 2 * columns, width), BF16),
            pltpu.SemaphoreType.DMA(()),
            pltpu.SemaphoreType.DMA((3,)),
        ],
        compiler_params=pltpu.CompilerParams(vmem_limit_bytes=16 << 20),
        cost_estimate=pl.CostEstimate(
            flops=12 * strip.size, bytes_accessed=2 * strip.size, transcendentals=0
        ),
        name="strip_statistics",
    )(in_hbm(crop_shift), in_hbm(strip), in_hbm(local_kernel), in_hbm(global_kernel))


def pack_body(local_ref, global_ref, *refs):
    vectors, (weight_out, affine_out, rows, sems) = refs[:-4], refs[-4:]
    channels = local_ref.shape[2]
    copies = []
    for i, vector in enumerate(vectors):
        copy = pltpu.make_async_copy(vector, rows.at[i], sems.at[i])
        copy.start()
        copies.append(copy)
    taps = [ref[t // 3, t % 3] for ref in (local_ref, global_ref) for t in range(9)]
    stacked = jnp.concatenate(taps, axis=0)
    for start in range(0, stacked.shape[0], LANES):
        weight_out[:, start : start + LANES] = stacked[start : start + LANES].T
    for copy in copies:
        copy.wait()
    table = [rows[i].reshape(1, channels) for i in range(len(vectors))]
    table.append(jnp.zeros((LANES - len(vectors), channels), F32))
    affine_out[...] = jnp.concatenate(table, axis=0).T


def pack_parameters(local_kernel, global_kernel, vectors):
    channels = local_kernel.shape[2]
    vmem = pl.BlockSpec(memory_space=pltpu.VMEM)
    return pl.pallas_call(
        pack_body,
        out_shape=(
            jax.ShapeDtypeStruct((channels, 18 * channels), BF16),
            jax.ShapeDtypeStruct((channels, LANES), F32),
        ),
        in_specs=[vmem] * 2 + [pl.BlockSpec(memory_space=pltpu.HBM)] * len(vectors),
        out_specs=(vmem, vmem),
        scratch_shapes=[
            pltpu.VMEM((len(vectors), channels), F32),
            pltpu.SemaphoreType.DMA((len(vectors),)),
        ],
        compiler_params=pltpu.CompilerParams(vmem_limit_bytes=12 << 20),
        cost_estimate=pl.CostEstimate(
            flops=0, bytes_accessed=8 * local_kernel.size, transcendentals=0
        ),
        name="pack_parameters",
    )(local_kernel, global_kernel, *[in_hbm(vector) for vector in vectors])


def main_body(
    dil_rows,
    group_size,
    image_cells,
    crop_shift,
    dilation_shift,
    x_ref,
    pair_ref,
    other_ref,
    total_ref,
    affine_ref,
    weight_ref,
    out_ref,
    crop_coef,
    image_coef,
    local_act,
    global_act,
    out_buf,
    out_sem,
):
    rows, channels, columns = x_ref.shape
    crops, used, width = lane_plan(columns, dil_rows)
    coef_lanes = -(-3 * used // LANES) * LANES
    sub_cols = columns // DILATION_COLUMNS
    first = lax.axis_index("rows") * rows
    sub_rows = image_cells // sub_cols
    split_row = split_of_strip(crop_shift[0], rows)
    split_col = jnp.remainder(crop_shift[1], CROP)
    image_row = jnp.remainder(dilation_shift[0], sub_rows)
    image_col = jnp.remainder(dilation_shift[1], sub_cols)

    def local_valid(row):
        return jnp.remainder(first + row - jnp.remainder(crop_shift[0], CROP) + CROP, CROP) != 0

    def global_valid(row):
        place = lax.div(first + row, dil_rows) - image_row + sub_rows
        return jnp.remainder(place, sub_rows) != 0

    lane = lax.broadcasted_iota(jnp.int32, (NORM_GROUPS, width), 1)
    inner = jnp.where(lane < used, lane, lane - used)
    total = total_ref[...]
    count = jnp.where(inner < 2 * crops, CROP * CROP * group_size, image_cells * group_size)
    average = total / count.astype(F32)
    square = pltpu.roll(average, width - used, 1)
    inverse = lax.rsqrt(jnp.maximum(square - average * average, 0.0) + EPSILON)
    moments = jnp.where(lane < used, average, pltpu.roll(inverse, used, 1))
    moments = jnp.where(lane < 2 * used, moments, 0.0)
    groups = group_selector((channels, 3 * NORM_GROUPS), 0, group_size)
    spread = jnp.dot(
        groups, jnp.concatenate(split3(moments), axis=0), preferred_element_type=F32
    )
    lane = lax.broadcasted_iota(jnp.int32, (channels, width), 1)
    at_crop = lane < 2 * crops
    gain = jnp.where(at_crop, affine_ref[:, 0:1], affine_ref[:, 2:3]) * 0.5
    bias = jnp.where(at_crop, affine_ref[:, 1:2], affine_ref[:, 3:4]) * 0.5
    scale = pltpu.roll(spread, width - used, 1) * gain
    shift = bias - spread * scale
    packed = []
    for value in (scale, shift):
        high, middle, low = split3(jnp.where(lane < used, value, 0.0))
        parts = [high.astype(F32), middle.astype(F32), low.astype(F32)]
        pad = coef_lanes - width
        if pad:
            parts = [
                jnp.concatenate([part, jnp.zeros((channels, pad), F32)], axis=1) for part in parts
            ]
        whole = parts[0] + pltpu.roll(parts[1], used, 1) + pltpu.roll(parts[2], 2 * used, 1)
        packed.append(whole.astype(BF16))
    selector_lane = lax.broadcasted_iota(jnp.int32, (coef_lanes, columns), 0)
    column = lax.broadcasted_iota(jnp.int32, (coef_lanes, columns), 1)
    selector_lane = jnp.where(
        selector_lane < used,
        selector_lane,
        jnp.where(
            selector_lane < 2 * used,
            selector_lane - used,
            jnp.where(selector_lane < 3 * used, selector_lane - 2 * used, width),
        ),
    )
    crop = crop_of(column, split_col, columns)
    chosen = [one_hot(selector_lane == crop + slot * crops) for slot in range(2)]
    phase = (column & (DILATION_COLUMNS - 1))[:, :LANES]
    for p in range(dil_rows):
        chosen.append(
            one_hot(selector_lane[:, :LANES] == phase + 2 * crops + p * DILATION_COLUMNS)
        )
    chosen = jnp.concatenate(chosen, axis=1)
    for k in range(2):
        table = jnp.dot(packed[k], chosen, preferred_element_type=F32)
        for slot in range(2):
            crop_coef[slot, k] = table[:, slot * columns : (slot + 1) * columns]
        for p in range(dil_rows):
            start = 2 * columns + p * LANES
            image_coef[p, k] = table[:, start : start + LANES]

    column = lax.broadcasted_iota(jnp.int32, (16, columns), 1)
    crop_col = (column - split_col) & (CROP - 1)
    image_q = (lax.shift_right_logical(column, 3) - image_col) & (sub_cols - 1)
    crop_left = one_hot(crop_col != 0)[:1]
    crop_right = one_hot(crop_col != CROP - 1)[:1]
    image_left = one_hot(image_q != 0)[:1]
    image_right = one_hot(image_q != sub_cols - 1)[:1]

    odd = (lax.axis_index("rows") & 1) == 1

    def source(row):
        if row < 0:
            row += dil_rows
            return jnp.where(odd, pair_ref[row], other_ref[row]).astype(F32)
        if row >= rows:
            row -= rows
            return jnp.where(odd, other_ref[row], pair_ref[row]).astype(F32)
        return x_ref[row].astype(F32)

    def store(target, half, step, mask_left, mask_right):
        act = (half + half * jnp.tanh(half)).astype(BF16)
        target[0:channels] = pltpu.roll(act, step, 1) * mask_left
        target[channels : 2 * channels] = act
        target[2 * channels :] = pltpu.roll(act, columns - step, 1) * mask_right

    def local_row(row):
        slot = jnp.where(min(max(row, 0), rows - 1) < split_row, 0, 1)
        half = source(row) * crop_coef[slot, 0] + crop_coef[slot, 1]
        store(local_act.at[row + 1], half, 1, crop_left, crop_right)

    def global_row(row):
        scale, shift = image_coef[row % dil_rows, 0], image_coef[row % dil_rows, 1]
        value = source(row)
        half = jnp.concatenate(
            [
                value[:, start : start + LANES] * scale + shift
                for start in range(0, columns, LANES)
            ],
            axis=1,
        )
        store(global_act.at[row + dil_rows], half, DILATION_COLUMNS, image_left, image_right)

    def taps(target, row, step, valid):
        zero = jnp.zeros((3 * channels, columns), BF16)
        return [
            jnp.where(valid(row), target[row], zero),
            target[row + step],
            jnp.where(valid(row + step), target[row + 2 * step], zero),
        ]

    offset = affine_ref[:, 4:5] + affine_ref[:, 5:6]
    done_local = -1
    done_global = -dil_rows
    copies = []
    for row in range(rows):
        while done_local <= row + 1:
            local_row(done_local)
            done_local += 1
        while done_global <= row + dil_rows:
            global_row(done_global)
            done_global += 1
        operand = jnp.concatenate(
            taps(local_act, row, 1, local_valid) + taps(global_act, row, dil_rows, global_valid),
            axis=0,
        )
        result = jnp.dot(weight_ref[...], operand, preferred_element_type=F32)
        out_buf[row] = (result + offset).astype(BF16)
        copy = pltpu.make_async_copy(out_buf.at[row], out_ref.at[row], out_sem.at[row])
        copy.start()
        copies.append(copy)
    for copy in copies:
        copy.wait()


def main_call(
    strip, pair, other, totals, affine, weights, crop_shift, dilation_shift
):
    rows, channels, columns = strip.shape
    dil_rows = pair.shape[0]
    smem = pl.BlockSpec(memory_space=pltpu.SMEM)
    vmem = pl.BlockSpec(memory_space=pltpu.VMEM)
    image_cells = (rows * lax.axis_size("rows") // dil_rows) * (columns // DILATION_COLUMNS)
    return pl.pallas_call(
        functools.partial(main_body, dil_rows, channels // NORM_GROUPS, image_cells),
        out_shape=jax.ShapeDtypeStruct(strip.shape, BF16),
        in_specs=[smem, smem] + [vmem] * 6,
        out_specs=pl.BlockSpec(memory_space=pl.ANY),
        scratch_shapes=[
            pltpu.VMEM((2, 2, channels, columns), F32),
            pltpu.VMEM((dil_rows, 2, channels, LANES), F32),
            pltpu.VMEM((rows + 2, 3 * channels, columns), BF16),
            pltpu.VMEM((rows + 2 * dil_rows, 3 * channels, columns), BF16),
            pltpu.VMEM(strip.shape, BF16),
            pltpu.SemaphoreType.DMA((rows,)),
        ],
        compiler_params=pltpu.CompilerParams(vmem_limit_bytes=32 << 20),
        cost_estimate=pl.CostEstimate(
            flops=36 * channels * strip.size,
            bytes_accessed=4 * strip.size,
            transcendentals=2 * strip.size,
        ),
        name="crop_and_dilated",
    )(crop_shift, dilation_shift, strip, pair, other, totals, affine, weights)


def shards(
    latent,
    crop_shift,
    dilation_shift,
    local_gain,
    local_bias,
    local_kernel,
    local_offset,
    global_gain,
    global_bias,
    global_kernel,
    global_offset,
):
    rows, columns, channels = latent.shape
    devices = lax.axis_size("rows")
    dil_rows = devices // DILATION_COLUMNS
    strip = latent.transpose(0, 2, 1)

    def shifted(value, step):
        return lax.ppermute(value, "rows", [(i, (i + step) % devices) for i in range(devices)])

    def exchanged(value, bit):
        return lax.ppermute(value, "rows", [(i, i ^ bit) for i in range(devices)])

    def paired(value, start):
        links = [(i % devices, (i + 1) % devices) for i in range(start, devices + start, 2)]
        return lax.ppermute(value, "rows", links + [(b, a) for a, b in links])

    totals, pair, other, local_kernel, global_kernel, strip = strip_statistics(
        strip, crop_shift, local_kernel, global_kernel, dil_rows
    )
    pair = paired(pair, 0)
    other = paired(other, 1)
    span = CROP // rows
    totals = totals + exchanged(totals, 1)
    own, swapped = totals[0], totals[1]
    above = shifted(swapped, span)
    below = shifted(swapped, -span)
    crops, used, width = lane_plan(columns, dil_rows)
    inner = jnp.arange(width, dtype=jnp.int32)
    inner = jnp.where(inner < used, inner, inner - used)
    if devices == 4 * span:
        image = (own + above) + (below + shifted(swapped, 2 * span))
    else:
        image = own
        bit = span
        while bit < devices:
            image = image + exchanged(image, bit)
            bit *= 2
    totals = own + jnp.where(inner < crops, above, below)
    totals = jnp.where(inner < 2 * crops, totals, image)
    totals, local_kernel = lax.optimization_barrier((totals, local_kernel))
    bit = 2
    while bit < span:
        totals = totals + exchanged(totals, bit)
        bit *= 2
    vectors = (local_gain, local_bias, global_gain, global_bias, local_offset, global_offset)
    weights, affine = pack_parameters(local_kernel, global_kernel, vectors)
    result = main_call(
        strip, pair, other, totals, affine, weights, crop_shift, dilation_shift
    )
    return result.transpose(0, 2, 1)


def solution(mesh):
    return jax.shard_map(
        shards,
        mesh=mesh,
        in_specs=(
            P(("groups", "rows"), None, None),
            P("groups"),
            P("groups"),
            P(),
            P(),
            P(),
            P(),
            P(),
            P(),
            P(),
            P(),
        ),
        out_specs=P(("groups", "rows"), None, None),
        check_vma=False,
    )
```

```python
import functools

import jax
import jax.numpy as jnp
from jax import lax
from jax.experimental import pallas as pl
from jax.experimental.pallas import tpu as pltpu
from jax.sharding import PartitionSpec as P

NORM_GROUPS = 32
DILATION_COLUMNS = 8
CROP = 32
EPSILON = 1e-05
LANES = 128

BF16 = jnp.bfloat16
F32 = jnp.float32


def split3(value):
    high = value.astype(BF16)
    rest = value - high.astype(F32)
    middle = rest.astype(BF16)
    low = (rest - middle.astype(F32)).astype(BF16)
    return high, middle, low


def in_hbm(value):
    return pltpu.with_memory_space_constraint(value, pltpu.HBM)


def one_hot(condition):
    return jnp.where(condition, 1.0, 0.0).astype(BF16)


def group_selector(shape, channel_dim, group_size):
    channel = lax.broadcasted_iota(jnp.int32, shape, channel_dim)
    first = (lax.broadcasted_iota(jnp.int32, shape, 1 - channel_dim) & 31) * group_size
    return one_hot((channel >= first) & (channel < first + group_size))


def lane_plan(columns, dil_rows):
    crops = columns // CROP
    used = 2 * crops + DILATION_COLUMNS * dil_rows
    return crops, used, -(-2 * used // LANES) * LANES


def crop_of(column, split_col, columns):
    return ((column - split_col) & (columns - 1)) // CROP


def split_of_strip(crop_shift, rows):
    first = lax.axis_index("rows") * rows
    return jnp.clip(jnp.remainder(crop_shift, CROP) - jnp.remainder(first, CROP), 0, rows)


def stats_body(
    dil_rows,
    group_size,
    shift_hbm,
    x_hbm,
    local_hbm,
    global_hbm,
    out_ref,
    pair_ref,
    other_ref,
    local_out,
    global_out,
    x_buf,
    crop_shift,
    selectors,
    shift_sem,
    sems,
):
    rows, channels, columns = x_buf.shape
    crops, used, width = lane_plan(columns, dil_rows)
    shift_copy = pltpu.make_async_copy(shift_hbm, crop_shift, shift_sem)
    shift_copy.start()
    copy = pltpu.make_async_copy(x_hbm, x_buf, sems.at[0])
    copy.start()
    later = [
        pltpu.make_async_copy(local_hbm, local_out, sems.at[1]),
        pltpu.make_async_copy(global_hbm, global_out, sems.at[2]),
    ]
    for kernel_copy in later:
        kernel_copy.start()
    shift_copy.wait()
    split_row = split_of_strip(crop_shift[0], rows)
    split_col = jnp.remainder(crop_shift[1], CROP)
    column = lax.broadcasted_iota(jnp.int32, (columns, width), 0)
    lane = lax.broadcasted_iota(jnp.int32, (columns, width), 1)
    crop_lane = lane - crop_of(column, split_col, columns)
    image_lane = lane - 2 * crops - (column & (DILATION_COLUMNS - 1))
    for slot in range(2):
        for p in range(dil_rows):
            for k in range(2):
                at_crop = crop_lane == slot * crops + k * used
                at_image = image_lane == p * DILATION_COLUMNS + k * used
                selectors[slot, p, k * columns : (k + 1) * columns] = one_hot(at_crop | at_image)
    groups = group_selector((NORM_GROUPS, channels), 1, group_size)
    copy.wait()
    odd = lax.axis_index("rows") & 1
    pair_ref[...] = x_buf[pl.ds(jnp.where(odd == 1, 0, rows - dil_rows), dil_rows)]
    other_ref[...] = x_buf[pl.ds(jnp.where(odd == 1, rows - dil_rows, 0), dil_rows)]
    total = None
    for r in range(rows):
        value = x_buf[r]
        wide = value.astype(F32)
        square = wide * wide
        high = square.astype(BF16)
        low = (square - high.astype(F32)).astype(BF16)
        slot = jnp.where(r < split_row, 0, 1)
        plain = selectors[slot, r % dil_rows, :columns]
        squares = selectors[slot, r % dil_rows, columns:]
        part = jnp.dot(
            jnp.concatenate([value, high, low], axis=1),
            jnp.concatenate([plain, squares, squares], axis=0),
            preferred_element_type=F32,
        )
        total = part if total is None else total + part
    high, middle, low = split3(total)
    parts = [jnp.dot(groups, part, preferred_element_type=F32) for part in (low, middle, high)]
    own = (parts[0] + parts[1]) + parts[2]
    lane = lax.broadcasted_iota(jnp.int32, (NORM_GROUPS, width), 1)
    inner = jnp.where(lane < used, lane, lane - used)
    upper = pltpu.roll(own, width - crops, 1)
    lower = pltpu.roll(own, crops, 1)
    out_ref[0] = own
    out_ref[1] = jnp.where(inner < crops, upper, jnp.where(inner < 2 * crops, lower, own))
    for kernel_copy in later:
        kernel_copy.wait()


def strip_statistics(strip, crop_shift, local_kernel, global_kernel, dil_rows):
    rows, channels, columns = strip.shape
    crops, used, width = lane_plan(columns, dil_rows)
    edge = jax.ShapeDtypeStruct((dil_rows, channels, columns), BF16)
    kernel = jax.ShapeDtypeStruct(local_kernel.shape, BF16)
    vmem = pl.BlockSpec(memory_space=pltpu.VMEM)
    return pl.pallas_call(
        functools.partial(stats_body, dil_rows, channels // NORM_GROUPS),
        out_shape=(
            jax.ShapeDtypeStruct((2, NORM_GROUPS, width), F32),
            edge,
            edge,
            kernel,
            kernel,
            jax.ShapeDtypeStruct(strip.shape, BF16),
        ),
        in_specs=[pl.BlockSpec(memory_space=pltpu.HBM)] * 4,
        out_specs=(vmem,) * 6,
        scratch_shapes=[
            pltpu.SMEM(crop_shift.shape, jnp.int32),
            pltpu.VMEM((2, dil_rows, 2 * columns, width), BF16),
            pltpu.SemaphoreType.DMA(()),
            pltpu.SemaphoreType.DMA((3,)),
        ],
        compiler_params=pltpu.CompilerParams(vmem_limit_bytes=16 << 20),
        cost_estimate=pl.CostEstimate(
            flops=12 * strip.size, bytes_accessed=2 * strip.size, transcendentals=0
        ),
        name="strip_statistics",
    )(in_hbm(crop_shift), in_hbm(strip), in_hbm(local_kernel), in_hbm(global_kernel))


def pack_body(local_ref, global_ref, *refs):
    vectors, (weight_out, affine_out, rows, sems) = refs[:-4], refs[-4:]
    channels = local_ref.shape[2]
    copies = []
    for i, vector in enumerate(vectors):
        copy = pltpu.make_async_copy(vector, rows.at[i], sems.at[i])
        copy.start()
        copies.append(copy)
    taps = [ref[t // 3, t % 3] for ref in (local_ref, global_ref) for t in range(9)]
    stacked = jnp.concatenate(taps, axis=0)
    for start in range(0, stacked.shape[0], LANES):
        weight_out[:, start : start + LANES] = stacked[start : start + LANES].T
    for copy in copies:
        copy.wait()
    table = [rows[i].reshape(1, channels) for i in range(len(vectors))]
    table.append(jnp.zeros((LANES - len(vectors), channels), F32))
    affine_out[...] = jnp.concatenate(table, axis=0).T


def pack_parameters(local_kernel, global_kernel, vectors):
    channels = local_kernel.shape[2]
    vmem = pl.BlockSpec(memory_space=pltpu.VMEM)
    return pl.pallas_call(
        pack_body,
        out_shape=(
            jax.ShapeDtypeStruct((channels, 18 * channels), BF16),
            jax.ShapeDtypeStruct((channels, LANES), F32),
        ),
        in_specs=[vmem] * 2 + [pl.BlockSpec(memory_space=pltpu.HBM)] * len(vectors),
        out_specs=(vmem, vmem),
        scratch_shapes=[
            pltpu.VMEM((len(vectors), channels), F32),
            pltpu.SemaphoreType.DMA((len(vectors),)),
        ],
        compiler_params=pltpu.CompilerParams(vmem_limit_bytes=12 << 20),
        cost_estimate=pl.CostEstimate(
            flops=0, bytes_accessed=8 * local_kernel.size, transcendentals=0
        ),
        name="pack_parameters",
    )(local_kernel, global_kernel, *[in_hbm(vector) for vector in vectors])


def main_body(
    dil_rows,
    group_size,
    image_cells,
    crop_shift,
    dilation_shift,
    x_ref,
    pair_ref,
    other_ref,
    total_ref,
    affine_ref,
    weight_ref,
    out_ref,
    crop_coef,
    image_coef,
    operand_ref,
    out_buf,
    out_sem,
):
    rows, channels, columns = x_ref.shape
    crops, used, width = lane_plan(columns, dil_rows)
    coef_lanes = -(-3 * used // LANES) * LANES
    sub_cols = columns // DILATION_COLUMNS
    first = lax.axis_index("rows") * rows
    sub_rows = image_cells // sub_cols
    split_row = split_of_strip(crop_shift[0], rows)
    split_col = jnp.remainder(crop_shift[1], CROP)
    image_row = jnp.remainder(dilation_shift[0], sub_rows)
    image_col = jnp.remainder(dilation_shift[1], sub_cols)

    def local_valid(row):
        return jnp.remainder(first + row - jnp.remainder(crop_shift[0], CROP) + CROP, CROP) != 0

    def global_valid(row):
        place = lax.div(first + row, dil_rows) - image_row + sub_rows
        return jnp.remainder(place, sub_rows) != 0

    lane = lax.broadcasted_iota(jnp.int32, (NORM_GROUPS, width), 1)
    inner = jnp.where(lane < used, lane, lane - used)
    total = total_ref[...]
    count = jnp.where(inner < 2 * crops, CROP * CROP * group_size, image_cells * group_size)
    average = total / count.astype(F32)
    square = pltpu.roll(average, width - used, 1)
    inverse = lax.rsqrt(jnp.maximum(square - average * average, 0.0) + EPSILON)
    moments = jnp.where(lane < used, average, pltpu.roll(inverse, used, 1))
    moments = jnp.where(lane < 2 * used, moments, 0.0)
    groups = group_selector((channels, 3 * NORM_GROUPS), 0, group_size)
    spread = jnp.dot(
        groups, jnp.concatenate(split3(moments), axis=0), preferred_element_type=F32
    )
    lane = lax.broadcasted_iota(jnp.int32, (channels, width), 1)
    at_crop = lane < 2 * crops
    gain = jnp.where(at_crop, affine_ref[:, 0:1], affine_ref[:, 2:3]) * 0.5
    bias = jnp.where(at_crop, affine_ref[:, 1:2], affine_ref[:, 3:4]) * 0.5
    scale = pltpu.roll(spread, width - used, 1) * gain
    shift = bias - spread * scale
    packed = []
    for value in (scale, shift):
        high, middle, low = split3(jnp.where(lane < used, value, 0.0))
        parts = [high.astype(F32), middle.astype(F32), low.astype(F32)]
        pad = coef_lanes - width
        if pad:
            parts = [
                jnp.concatenate([part, jnp.zeros((channels, pad), F32)], axis=1) for part in parts
            ]
        whole = parts[0] + pltpu.roll(parts[1], used, 1) + pltpu.roll(parts[2], 2 * used, 1)
        packed.append(whole.astype(BF16))
    selector_lane = lax.broadcasted_iota(jnp.int32, (coef_lanes, columns), 0)
    column = lax.broadcasted_iota(jnp.int32, (coef_lanes, columns), 1)
    selector_lane = jnp.where(
        selector_lane < used,
        selector_lane,
        jnp.where(
            selector_lane < 2 * used,
            selector_lane - used,
            jnp.where(selector_lane < 3 * used, selector_lane - 2 * used, width),
        ),
    )
    crop = crop_of(column, split_col, columns)
    chosen = [one_hot(selector_lane == crop + slot * crops) for slot in range(2)]
    phase = (column & (DILATION_COLUMNS - 1))[:, :LANES]
    for p in range(dil_rows):
        chosen.append(
            one_hot(selector_lane[:, :LANES] == phase + 2 * crops + p * DILATION_COLUMNS)
        )
    chosen = jnp.concatenate(chosen, axis=1)
    for k in range(2):
        table = jnp.dot(packed[k], chosen, preferred_element_type=F32)
        for slot in range(2):
            crop_coef[slot, k] = table[:, slot * columns : (slot + 1) * columns]
        for p in range(dil_rows):
            start = 2 * columns + p * LANES
            image_coef[p, k] = table[:, start : start + LANES]

    column = lax.broadcasted_iota(jnp.int32, (16, columns), 1)
    crop_col = (column - split_col) & (CROP - 1)
    image_q = (lax.shift_right_logical(column, 3) - image_col) & (sub_cols - 1)
    crop_left = one_hot(crop_col != 0)[:1]
    crop_right = one_hot(crop_col != CROP - 1)[:1]
    image_left = one_hot(image_q != 0)[:1]
    image_right = one_hot(image_q != sub_cols - 1)[:1]

    odd = (lax.axis_index("rows") & 1) == 1

    def source(row):
        if row < 0:
            row += dil_rows
            return jnp.where(odd, pair_ref[row], other_ref[row]).astype(F32)
        if row >= rows:
            row -= rows
            return jnp.where(odd, other_ref[row], pair_ref[row]).astype(F32)
        return x_ref[row].astype(F32)

    def flag(valid):
        return jnp.where(valid, jnp.ones((16, columns), F32), 0.0).astype(BF16)[:1]

    def spread(base, row, step, shift, half, mask_left, mask_right, valid):
        act = (half + half * jnp.tanh(half)).astype(BF16)
        from_left = pltpu.roll(act, shift, 1)
        from_right = pltpu.roll(act, columns - shift, 1)
        for tap, target in ((0, row + step), (1, row), (2, row - step)):
            if not 0 <= target < rows:
                continue
            start = base + tap * 3 * channels
            left, centre, right = mask_left, act, mask_right
            if tap != 1:
                counts = flag(valid(target if tap == 0 else row))
                left, centre, right = left * counts, act * counts, right * counts
            operand_ref[target, start : start + channels] = from_left * left
            operand_ref[target, start + channels : start + 2 * channels] = centre
            operand_ref[target, start + 2 * channels : start + 3 * channels] = from_right * right

    def local_row(row):
        slot = jnp.where(min(max(row, 0), rows - 1) < split_row, 0, 1)
        half = source(row) * crop_coef[slot, 0] + crop_coef[slot, 1]
        spread(0, row, 1, 1, half, crop_left, crop_right, local_valid)

    def global_row(row):
        scale, shift = image_coef[row % dil_rows, 0], image_coef[row % dil_rows, 1]
        value = source(row)
        half = jnp.concatenate(
            [
                value[:, start : start + LANES] * scale + shift
                for start in range(0, columns, LANES)
            ],
            axis=1,
        )
        base = 9 * channels
        spread(
            base, row, dil_rows, DILATION_COLUMNS, half, image_left, image_right, global_valid
        )

    offset = affine_ref[:, 4:5] + affine_ref[:, 5:6]
    done_local = -1
    done_global = -dil_rows
    copies = []
    for row in range(rows):
        while done_local <= row + 1:
            local_row(done_local)
            done_local += 1
        while done_global <= row + dil_rows:
            global_row(done_global)
            done_global += 1
        result = jnp.dot(weight_ref[...], operand_ref[row], preferred_element_type=F32)
        out_buf[row] = (result + offset).astype(BF16)
        copy = pltpu.make_async_copy(out_buf.at[row], out_ref.at[row], out_sem.at[row])
        copy.start()
        copies.append(copy)
    for copy in copies:
        copy.wait()


def main_call(
    strip, pair, other, totals, affine, weights, crop_shift, dilation_shift
):
    rows, channels, columns = strip.shape
    dil_rows = pair.shape[0]
    smem = pl.BlockSpec(memory_space=pltpu.SMEM)
    vmem = pl.BlockSpec(memory_space=pltpu.VMEM)
    image_cells = (rows * lax.axis_size("rows") // dil_rows) * (columns // DILATION_COLUMNS)
    return pl.pallas_call(
        functools.partial(main_body, dil_rows, channels // NORM_GROUPS, image_cells),
        out_shape=jax.ShapeDtypeStruct(strip.shape, BF16),
        in_specs=[smem, smem] + [vmem] * 6,
        out_specs=pl.BlockSpec(memory_space=pl.ANY),
        scratch_shapes=[
            pltpu.VMEM((2, 2, channels, columns), F32),
            pltpu.VMEM((dil_rows, 2, channels, LANES), F32),
            pltpu.VMEM((rows, 18 * channels, columns), BF16),
            pltpu.VMEM(strip.shape, BF16),
            pltpu.SemaphoreType.DMA((rows,)),
        ],
        compiler_params=pltpu.CompilerParams(vmem_limit_bytes=40 << 20),
        cost_estimate=pl.CostEstimate(
            flops=36 * channels * strip.size,
            bytes_accessed=4 * strip.size,
            transcendentals=2 * strip.size,
        ),
        name="crop_and_dilated",
    )(crop_shift, dilation_shift, strip, pair, other, totals, affine, weights)


def shards(
    latent,
    crop_shift,
    dilation_shift,
    local_gain,
    local_bias,
    local_kernel,
    local_offset,
    global_gain,
    global_bias,
    global_kernel,
    global_offset,
):
    rows, columns, channels = latent.shape
    devices = lax.axis_size("rows")
    dil_rows = devices // DILATION_COLUMNS
    strip = latent.transpose(0, 2, 1)

    def shifted(value, step):
        return lax.ppermute(value, "rows", [(i, (i + step) % devices) for i in range(devices)])

    def exchanged(value, bit):
        return lax.ppermute(value, "rows", [(i, i ^ bit) for i in range(devices)])

    def paired(value, start):
        links = [(i % devices, (i + 1) % devices) for i in range(start, devices + start, 2)]
        return lax.ppermute(value, "rows", links + [(b, a) for a, b in links])

    totals, pair, other, local_kernel, global_kernel, strip = strip_statistics(
        strip, crop_shift, local_kernel, global_kernel, dil_rows
    )
    pair = paired(pair, 0)
    other = paired(other, 1)
    span = CROP // rows
    totals = totals + exchanged(totals, 1)
    own, swapped = totals[0], totals[1]
    above = shifted(swapped, span)
    below = shifted(swapped, -span)
    crops, used, width = lane_plan(columns, dil_rows)
    inner = jnp.arange(width, dtype=jnp.int32)
    inner = jnp.where(inner < used, inner, inner - used)
    if devices == 4 * span:
        image = (own + above) + (below + shifted(swapped, 2 * span))
    else:
        image = own
        bit = span
        while bit < devices:
            image = image + exchanged(image, bit)
            bit *= 2
    totals = own + jnp.where(inner < crops, above, below)
    totals = jnp.where(inner < 2 * crops, totals, image)
    totals, local_kernel = lax.optimization_barrier((totals, local_kernel))
    bit = 2
    while bit < span:
        totals = totals + exchanged(totals, bit)
        bit *= 2
    vectors = (local_gain, local_bias, global_gain, global_bias, local_offset, global_offset)
    weights, affine = pack_parameters(local_kernel, global_kernel, vectors)
    result = main_call(
        strip, pair, other, totals, affine, weights, crop_shift, dilation_shift
    )
    return result.transpose(0, 2, 1)


def solution(mesh):
    return jax.shard_map(
        shards,
        mesh=mesh,
        in_specs=(
            P(("groups", "rows"), None, None),
            P("groups"),
            P("groups"),
            P(),
            P(),
            P(),
            P(),
            P(),
            P(),
            P(),
            P(),
        ),
        out_specs=P(("groups", "rows"), None, None),
        check_vma=False,
    )
```

```python
import functools

import jax
import jax.numpy as jnp
from jax import lax
from jax.experimental import pallas as pl
from jax.experimental.pallas import tpu as pltpu
from jax.sharding import PartitionSpec as P

NORM_GROUPS = 32
DILATION_COLUMNS = 8
CROP = 32
EPSILON = 1e-05
LANES = 128

BF16 = jnp.bfloat16
F32 = jnp.float32


def split3(value):
    high = value.astype(BF16)
    rest = value - high.astype(F32)
    middle = rest.astype(BF16)
    low = (rest - middle.astype(F32)).astype(BF16)
    return high, middle, low


def in_hbm(value):
    return pltpu.with_memory_space_constraint(value, pltpu.HBM)


def one_hot(condition):
    return jnp.where(condition, 1.0, 0.0).astype(BF16)


def group_selector(shape, channel_dim, group_size):
    channel = lax.broadcasted_iota(jnp.int32, shape, channel_dim)
    first = (lax.broadcasted_iota(jnp.int32, shape, 1 - channel_dim) & 31) * group_size
    return one_hot((channel >= first) & (channel < first + group_size))


def lane_plan(columns, dil_rows):
    crops = columns // CROP
    used = 2 * crops + DILATION_COLUMNS * dil_rows
    return crops, used, -(-2 * used // LANES) * LANES


def crop_of(column, split_col, columns):
    return ((column - split_col) & (columns - 1)) // CROP


def split_of_strip(crop_shift, rows):
    first = lax.axis_index("rows") * rows
    return jnp.clip(jnp.remainder(crop_shift, CROP) - jnp.remainder(first, CROP), 0, rows)


def stats_body(
    dil_rows,
    group_size,
    shift_hbm,
    x_hbm,
    local_hbm,
    global_hbm,
    out_ref,
    pair_ref,
    other_ref,
    local_out,
    global_out,
    x_buf,
    side_ref,
    crop_shift,
    selectors,
    shift_sem,
    sems,
):
    rows, channels, columns = x_buf.shape
    crops, used, width = lane_plan(columns, dil_rows)
    shift_copy = pltpu.make_async_copy(shift_hbm, crop_shift, shift_sem)
    shift_copy.start()
    copy = pltpu.make_async_copy(x_hbm, x_buf, sems.at[0])
    copy.start()
    later = [
        pltpu.make_async_copy(local_hbm, local_out, sems.at[1]),
        pltpu.make_async_copy(global_hbm, global_out, sems.at[2]),
    ]
    for kernel_copy in later:
        kernel_copy.start()
    shift_copy.wait()
    split_row = split_of_strip(crop_shift[0], rows)
    split_col = jnp.remainder(crop_shift[1], CROP)
    column = lax.broadcasted_iota(jnp.int32, (columns, width), 0)
    lane = lax.broadcasted_iota(jnp.int32, (columns, width), 1)
    crop_lane = lane - crop_of(column, split_col, columns)
    image_lane = lane - 2 * crops - (column & (DILATION_COLUMNS - 1))
    for slot in range(2):
        for p in range(dil_rows):
            for k in range(2):
                at_crop = crop_lane == slot * crops + k * used
                at_image = image_lane == p * DILATION_COLUMNS + k * used
                selectors[slot, p, k * columns : (k + 1) * columns] = one_hot(at_crop | at_image)
    groups = group_selector((NORM_GROUPS, channels), 1, group_size)
    copy.wait()
    odd = lax.axis_index("rows") & 1
    pair_ref[...] = x_buf[pl.ds(jnp.where(odd == 1, 0, rows - dil_rows), dil_rows)]
    other_ref[...] = x_buf[pl.ds(jnp.where(odd == 1, rows - dil_rows, 0), dil_rows)]
    left, right = [], []
    for r in range(rows):
        value = x_buf[r]
        wide = value.astype(F32)
        square = wide * wide
        high = square.astype(BF16)
        low = (square - high.astype(F32)).astype(BF16)
        slot = jnp.where(r < split_row, 0, 1)
        plain = selectors[slot, r % dil_rows, :columns]
        squares = selectors[slot, r % dil_rows, columns:]
        left.extend([value, high, low])
        right.extend([plain, squares, squares])
    total = jnp.dot(
        jnp.concatenate(left, axis=1),
        jnp.concatenate(right, axis=0),
        preferred_element_type=F32,
    )
    high, middle, low = split3(total)
    parts = [jnp.dot(groups, part, preferred_element_type=F32) for part in (low, middle, high)]
    own = (parts[0] + parts[1]) + parts[2]
    lane = lax.broadcasted_iota(jnp.int32, (NORM_GROUPS, width), 1)
    inner = jnp.where(lane < used, lane, lane - used)
    upper = pltpu.roll(own, width - crops, 1)
    lower = pltpu.roll(own, crops, 1)
    out_ref[0] = own
    out_ref[1] = jnp.where(inner < crops, upper, jnp.where(inner < 2 * crops, lower, own))
    odd = lax.div(lax.axis_index("rows"), CROP // rows) & 1
    near = jnp.where(inner < crops, odd, jnp.where(inner < 2 * crops, 1 - odd, 1))
    side_ref[0] = near.astype(F32)
    side_ref[1] = jnp.where(inner < 2 * crops, 1 - near, 1).astype(F32)
    for kernel_copy in later:
        kernel_copy.wait()


def strip_statistics(strip, crop_shift, local_kernel, global_kernel, dil_rows):
    rows, channels, columns = strip.shape
    crops, used, width = lane_plan(columns, dil_rows)
    edge = jax.ShapeDtypeStruct((dil_rows, channels, columns), BF16)
    kernel = jax.ShapeDtypeStruct(local_kernel.shape, BF16)
    vmem = pl.BlockSpec(memory_space=pltpu.VMEM)
    return pl.pallas_call(
        functools.partial(stats_body, dil_rows, channels // NORM_GROUPS),
        out_shape=(
            jax.ShapeDtypeStruct((2, NORM_GROUPS, width), F32),
            edge,
            edge,
            kernel,
            kernel,
            jax.ShapeDtypeStruct(strip.shape, BF16),
            jax.ShapeDtypeStruct((2, NORM_GROUPS, width), F32),
        ),
        in_specs=[pl.BlockSpec(memory_space=pltpu.HBM)] * 4,
        out_specs=(vmem,) * 7,
        scratch_shapes=[
            pltpu.SMEM(crop_shift.shape, jnp.int32),
            pltpu.VMEM((2, dil_rows, 2 * columns, width), BF16),
            pltpu.SemaphoreType.DMA(()),
            pltpu.SemaphoreType.DMA((3,)),
        ],
        compiler_params=pltpu.CompilerParams(vmem_limit_bytes=16 << 20),
        cost_estimate=pl.CostEstimate(
            flops=12 * strip.size, bytes_accessed=2 * strip.size, transcendentals=0
        ),
        name="strip_statistics",
    )(in_hbm(crop_shift), in_hbm(strip), in_hbm(local_kernel), in_hbm(global_kernel))


def pack_body(local_ref, global_ref, *refs):
    vectors, (weight_out, affine_out, rows, sems) = refs[:-4], refs[-4:]
    channels = local_ref.shape[2]
    copies = []
    for i, vector in enumerate(vectors):
        copy = pltpu.make_async_copy(vector, rows.at[i], sems.at[i])
        copy.start()
        copies.append(copy)
    taps = [ref[t // 3, t % 3] for ref in (local_ref, global_ref) for t in range(9)]
    stacked = jnp.concatenate(taps, axis=0)
    for start in range(0, stacked.shape[0], LANES):
        weight_out[:, start : start + LANES] = stacked[start : start + LANES].T
    for copy in copies:
        copy.wait()
    table = [rows[i].reshape(1, channels) for i in range(len(vectors))]
    table.append(jnp.zeros((LANES - len(vectors), channels), F32))
    affine_out[...] = jnp.concatenate(table, axis=0).T


def pack_parameters(local_kernel, global_kernel, vectors):
    channels = local_kernel.shape[2]
    vmem = pl.BlockSpec(memory_space=pltpu.VMEM)
    return pl.pallas_call(
        pack_body,
        out_shape=(
            jax.ShapeDtypeStruct((channels, 18 * channels), BF16),
            jax.ShapeDtypeStruct((channels, LANES), F32),
        ),
        in_specs=[vmem] * 2 + [pl.BlockSpec(memory_space=pltpu.HBM)] * len(vectors),
        out_specs=(vmem, vmem),
        scratch_shapes=[
            pltpu.VMEM((len(vectors), channels), F32),
            pltpu.SemaphoreType.DMA((len(vectors),)),
        ],
        compiler_params=pltpu.CompilerParams(vmem_limit_bytes=12 << 20),
        cost_estimate=pl.CostEstimate(
            flops=0, bytes_accessed=8 * local_kernel.size, transcendentals=0
        ),
        name="pack_parameters",
    )(local_kernel, global_kernel, *[in_hbm(vector) for vector in vectors])


def main_body(
    dil_rows,
    group_size,
    image_cells,
    crop_shift,
    dilation_shift,
    x_ref,
    pair_ref,
    other_ref,
    total_ref,
    affine_ref,
    weight_ref,
    out_ref,
    crop_coef,
    image_coef,
    operand_ref,
    out_buf,
    out_sem,
):
    rows, channels, columns = x_ref.shape
    crops, used, width = lane_plan(columns, dil_rows)
    coef_lanes = -(-3 * used // LANES) * LANES
    sub_cols = columns // DILATION_COLUMNS
    first = lax.axis_index("rows") * rows
    sub_rows = image_cells // sub_cols
    split_row = split_of_strip(crop_shift[0], rows)
    split_col = jnp.remainder(crop_shift[1], CROP)
    image_row = jnp.remainder(dilation_shift[0], sub_rows)
    image_col = jnp.remainder(dilation_shift[1], sub_cols)

    def local_valid(row):
        return jnp.remainder(first + row - jnp.remainder(crop_shift[0], CROP) + CROP, CROP) != 0

    def global_valid(row):
        place = lax.div(first + row, dil_rows) - image_row + sub_rows
        return jnp.remainder(place, sub_rows) != 0

    lane = lax.broadcasted_iota(jnp.int32, (NORM_GROUPS, width), 1)
    inner = jnp.where(lane < used, lane, lane - used)
    total = total_ref[...]
    count = jnp.where(inner < 2 * crops, CROP * CROP * group_size, image_cells * group_size)
    average = total / count.astype(F32)
    square = pltpu.roll(average, width - used, 1)
    inverse = lax.rsqrt(jnp.maximum(square - average * average, 0.0) + EPSILON)
    moments = jnp.where(lane < used, average, pltpu.roll(inverse, used, 1))
    moments = jnp.where(lane < 2 * used, moments, 0.0)
    groups = group_selector((channels, 3 * NORM_GROUPS), 0, group_size)
    spread = jnp.dot(
        groups, jnp.concatenate(split3(moments), axis=0), preferred_element_type=F32
    )
    lane = lax.broadcasted_iota(jnp.int32, (channels, width), 1)
    at_crop = lane < 2 * crops
    gain = jnp.where(at_crop, affine_ref[:, 0:1], affine_ref[:, 2:3]) * 0.5
    bias = jnp.where(at_crop, affine_ref[:, 1:2], affine_ref[:, 3:4]) * 0.5
    scale = pltpu.roll(spread, width - used, 1) * gain
    shift = bias - spread * scale
    packed = []
    for value in (scale, shift):
        high, middle, low = split3(jnp.where(lane < used, value, 0.0))
        parts = [high.astype(F32), middle.astype(F32), low.astype(F32)]
        pad = coef_lanes - width
        if pad:
            parts = [
                jnp.concatenate([part, jnp.zeros((channels, pad), F32)], axis=1) for part in parts
            ]
        whole = parts[0] + pltpu.roll(parts[1], used, 1) + pltpu.roll(parts[2], 2 * used, 1)
        packed.append(whole.astype(BF16))
    selector_lane = lax.broadcasted_iota(jnp.int32, (coef_lanes, columns), 0)
    column = lax.broadcasted_iota(jnp.int32, (coef_lanes, columns), 1)
    selector_lane = jnp.where(
        selector_lane < used,
        selector_lane,
        jnp.where(
            selector_lane < 2 * used,
            selector_lane - used,
            jnp.where(selector_lane < 3 * used, selector_lane - 2 * used, width),
        ),
    )
    crop = crop_of(column, split_col, columns)
    chosen = [one_hot(selector_lane == crop + slot * crops) for slot in range(2)]
    phase = (column & (DILATION_COLUMNS - 1))[:, :LANES]
    for p in range(dil_rows):
        chosen.append(
            one_hot(selector_lane[:, :LANES] == phase + 2 * crops + p * DILATION_COLUMNS)
        )
    chosen = jnp.concatenate(chosen, axis=1)
    for k in range(2):
        table = jnp.dot(packed[k], chosen, preferred_element_type=F32)
        for slot in range(2):
            crop_coef[slot, k] = table[:, slot * columns : (slot + 1) * columns]
        for p in range(dil_rows):
            start = 2 * columns + p * LANES
            image_coef[p, k] = table[:, start : start + LANES]

    column = lax.broadcasted_iota(jnp.int32, (16, columns), 1)
    crop_col = (column - split_col) & (CROP - 1)
    image_q = (lax.shift_right_logical(column, 3) - image_col) & (sub_cols - 1)
    crop_left = one_hot(crop_col != 0)[:1]
    crop_right = one_hot(crop_col != CROP - 1)[:1]
    image_left = one_hot(image_q != 0)[:1]
    image_right = one_hot(image_q != sub_cols - 1)[:1]

    odd = (lax.axis_index("rows") & 1) == 1

    def source(row):
        if row < 0:
            row += dil_rows
            return jnp.where(odd, pair_ref[row], other_ref[row]).astype(F32)
        if row >= rows:
            row -= rows
            return jnp.where(odd, other_ref[row], pair_ref[row]).astype(F32)
        return x_ref[row].astype(F32)

    def flag(valid):
        return jnp.where(valid, jnp.ones((16, columns), F32), 0.0).astype(BF16)[:1]

    def spread(base, row, step, shift, half, mask_left, mask_right, valid):
        act = (half + half * jnp.tanh(half)).astype(BF16)
        from_left = pltpu.roll(act, shift, 1)
        from_right = pltpu.roll(act, columns - shift, 1)
        for tap, target in ((0, row + step), (1, row), (2, row - step)):
            if not 0 <= target < rows:
                continue
            start = base + tap * 3 * channels
            left, centre, right = mask_left, act, mask_right
            if tap != 1:
                counts = flag(valid(target if tap == 0 else row))
                left, centre, right = left * counts, act * counts, right * counts
            operand_ref[target, start : start + channels] = from_left * left
            operand_ref[target, start + channels : start + 2 * channels] = centre
            operand_ref[target, start + 2 * channels : start + 3 * channels] = from_right * right

    def local_row(row):
        slot = jnp.where(min(max(row, 0), rows - 1) < split_row, 0, 1)
        half = source(row) * crop_coef[slot, 0] + crop_coef[slot, 1]
        spread(0, row, 1, 1, half, crop_left, crop_right, local_valid)

    def global_row(row):
        scale, shift = image_coef[row % dil_rows, 0], image_coef[row % dil_rows, 1]
        value = source(row)
        half = jnp.concatenate(
            [
                value[:, start : start + LANES] * scale + shift
                for start in range(0, columns, LANES)
            ],
            axis=1,
        )
        base = 9 * channels
        spread(
            base, row, dil_rows, DILATION_COLUMNS, half, image_left, image_right, global_valid
        )

    offset = affine_ref[:, 4:5] + affine_ref[:, 5:6]
    done_local = -1
    done_global = -dil_rows
    copies = []
    for row in range(rows):
        reach = min(row + 1, rows - 1)
        while done_local <= reach + 1:
            local_row(done_local)
            done_local += 1
        while done_global <= reach + dil_rows:
            global_row(done_global)
            done_global += 1
        result = jnp.dot(weight_ref[...], operand_ref[row], preferred_element_type=F32)
        out_buf[row] = (result + offset).astype(BF16)
        copy = pltpu.make_async_copy(out_buf.at[row], out_ref.at[row], out_sem.at[row])
        copy.start()
        copies.append(copy)
    for copy in copies:
        copy.wait()


def main_call(
    strip, pair, other, totals, affine, weights, crop_shift, dilation_shift
):
    rows, channels, columns = strip.shape
    dil_rows = pair.shape[0]
    smem = pl.BlockSpec(memory_space=pltpu.SMEM)
    vmem = pl.BlockSpec(memory_space=pltpu.VMEM)
    image_cells = (rows * lax.axis_size("rows") // dil_rows) * (columns // DILATION_COLUMNS)
    return pl.pallas_call(
        functools.partial(main_body, dil_rows, channels // NORM_GROUPS, image_cells),
        out_shape=jax.ShapeDtypeStruct(strip.shape, BF16),
        in_specs=[smem, smem] + [vmem] * 6,
        out_specs=pl.BlockSpec(memory_space=pl.ANY),
        scratch_shapes=[
            pltpu.VMEM((2, 2, channels, columns), F32),
            pltpu.VMEM((dil_rows, 2, channels, LANES), F32),
            pltpu.VMEM((rows, 18 * channels, columns), BF16),
            pltpu.VMEM(strip.shape, BF16),
            pltpu.SemaphoreType.DMA((rows,)),
        ],
        compiler_params=pltpu.CompilerParams(vmem_limit_bytes=40 << 20),
        cost_estimate=pl.CostEstimate(
            flops=36 * channels * strip.size,
            bytes_accessed=4 * strip.size,
            transcendentals=2 * strip.size,
        ),
        name="crop_and_dilated",
    )(crop_shift, dilation_shift, strip, pair, other, totals, affine, weights)


def shards(
    latent,
    crop_shift,
    dilation_shift,
    local_gain,
    local_bias,
    local_kernel,
    local_offset,
    global_gain,
    global_bias,
    global_kernel,
    global_offset,
):
    rows, columns, channels = latent.shape
    devices = lax.axis_size("rows")
    dil_rows = devices // DILATION_COLUMNS
    strip = latent.transpose(0, 2, 1)

    def shifted(value, step):
        return lax.ppermute(value, "rows", [(i, (i + step) % devices) for i in range(devices)])

    def exchanged(value, bit):
        return lax.ppermute(value, "rows", [(i, i ^ bit) for i in range(devices)])

    def paired(value, start):
        links = [(i % devices, (i + 1) % devices) for i in range(start, devices + start, 2)]
        return lax.ppermute(value, "rows", links + [(b, a) for a, b in links])

    totals, pair, other, local_kernel, global_kernel, strip, side = strip_statistics(
        strip, crop_shift, local_kernel, global_kernel, dil_rows
    )
    pair = paired(pair, 0)
    other = paired(other, 1)
    span = CROP // rows
    totals = totals + exchanged(totals, 1)
    own, swapped = totals[0], totals[1]
    crops, used, width = lane_plan(columns, dil_rows)
    inner = jnp.arange(width, dtype=jnp.int32)
    inner = jnp.where(inner < used, inner, inner - used)
    if devices == 4 * span:
        near = exchanged(swapped, span)
        across = exchanged(swapped, 2 * span)
        third = exchanged(swapped, 3 * span)
        totals = (own + side[0] * near) + side[1] * third
        totals = totals + jnp.where(inner < 2 * crops, 0.0, across)
    else:
        above = shifted(swapped, span)
        below = shifted(swapped, -span)
        image = own
        bit = span
        while bit < devices:
            image = image + exchanged(image, bit)
            bit *= 2
        totals = own + jnp.where(inner < crops, above, below)
        totals = jnp.where(inner < 2 * crops, totals, image)
    totals, local_kernel = lax.optimization_barrier((totals, local_kernel))
    bit = 2
    while bit < span:
        totals = totals + exchanged(totals, bit)
        bit *= 2
    vectors = (local_gain, local_bias, global_gain, global_bias, local_offset, global_offset)
    weights, affine = pack_parameters(local_kernel, global_kernel, vectors)
    result = main_call(
        strip, pair, other, totals, affine, weights, crop_shift, dilation_shift
    )
    return result.transpose(0, 2, 1)


def solution(mesh):
    return jax.shard_map(
        shards,
        mesh=mesh,
        in_specs=(
            P(("groups", "rows"), None, None),
            P("groups"),
            P("groups"),
            P(),
            P(),
            P(),
            P(),
            P(),
            P(),
            P(),
            P(),
        ),
        out_specs=P(("groups", "rows"), None, None),
        check_vma=False,
    )
```

```python
import functools

import jax
import jax.numpy as jnp
from jax import lax
from jax.experimental import pallas as pl
from jax.experimental.pallas import tpu as pltpu
from jax.sharding import PartitionSpec as P

NORM_GROUPS = 32
DILATION_COLUMNS = 8
CROP = 32
EPSILON = 1e-05
LANES = 128

BF16 = jnp.bfloat16
F32 = jnp.float32


def split3(value):
    high = value.astype(BF16)
    rest = value - high.astype(F32)
    middle = rest.astype(BF16)
    low = (rest - middle.astype(F32)).astype(BF16)
    return high, middle, low


def in_hbm(value):
    return pltpu.with_memory_space_constraint(value, pltpu.HBM)


def one_hot(condition):
    return jnp.where(condition, 1.0, 0.0).astype(BF16)


def group_selector(shape, channel_dim, group_size):
    channel = lax.broadcasted_iota(jnp.int32, shape, channel_dim)
    first = (lax.broadcasted_iota(jnp.int32, shape, 1 - channel_dim) & 31) * group_size
    return one_hot((channel >= first) & (channel < first + group_size))


def lane_plan(columns, dil_rows):
    crops = columns // CROP
    used = 2 * crops + DILATION_COLUMNS * dil_rows
    return crops, used, -(-2 * used // LANES) * LANES


def crop_of(column, split_col, columns):
    return ((column - split_col) & (columns - 1)) // CROP


def split_of_strip(crop_shift, rows):
    first = lax.axis_index("rows") * rows
    return jnp.clip(jnp.remainder(crop_shift, CROP) - jnp.remainder(first, CROP), 0, rows)


def stats_body(
    dil_rows,
    group_size,
    shift_hbm,
    x_hbm,
    local_hbm,
    global_hbm,
    out_ref,
    pair_ref,
    other_ref,
    local_out,
    global_out,
    x_buf,
    side_ref,
    crop_shift,
    selectors,
    shift_sem,
    sems,
):
    rows, channels, columns = x_buf.shape
    crops, used, width = lane_plan(columns, dil_rows)
    shift_copy = pltpu.make_async_copy(shift_hbm, crop_shift, shift_sem)
    shift_copy.start()
    copy = pltpu.make_async_copy(x_hbm, x_buf, sems.at[0])
    copy.start()
    later = [
        pltpu.make_async_copy(local_hbm, local_out, sems.at[1]),
        pltpu.make_async_copy(global_hbm, global_out, sems.at[2]),
    ]
    for kernel_copy in later:
        kernel_copy.start()
    shift_copy.wait()
    split_row = split_of_strip(crop_shift[0], rows)
    split_col = jnp.remainder(crop_shift[1], CROP)
    column = lax.broadcasted_iota(jnp.int32, (columns, width), 0)
    lane = lax.broadcasted_iota(jnp.int32, (columns, width), 1)
    crop_lane = lane - crop_of(column, split_col, columns)
    image_lane = lane - 2 * crops - (column & (DILATION_COLUMNS - 1))
    for slot in range(2):
        for p in range(dil_rows):
            for k in range(2):
                at_crop = crop_lane == slot * crops + k * used
                at_image = image_lane == p * DILATION_COLUMNS + k * used
                selectors[slot, p, k * columns : (k + 1) * columns] = one_hot(at_crop | at_image)
    groups = group_selector((NORM_GROUPS, channels), 1, group_size)
    copy.wait()
    odd = lax.axis_index("rows") & 1
    pair_ref[...] = x_buf[pl.ds(jnp.where(odd == 1, 0, rows - dil_rows), dil_rows)]
    other_ref[...] = x_buf[pl.ds(jnp.where(odd == 1, rows - dil_rows, 0), dil_rows)]
    left, right = [], []
    for r in range(rows):
        value = x_buf[r]
        wide = value.astype(F32)
        square = wide * wide
        high = square.astype(BF16)
        low = (square - high.astype(F32)).astype(BF16)
        slot = jnp.where(r < split_row, 0, 1)
        plain = selectors[slot, r % dil_rows, :columns]
        squares = selectors[slot, r % dil_rows, columns:]
        left.extend([value, high, low])
        right.extend([plain, squares, squares])
    total = jnp.dot(
        jnp.concatenate(left, axis=1),
        jnp.concatenate(right, axis=0),
        preferred_element_type=F32,
    )
    high, middle, low = split3(total)
    parts = [jnp.dot(groups, part, preferred_element_type=F32) for part in (low, middle, high)]
    own = (parts[0] + parts[1]) + parts[2]
    lane = lax.broadcasted_iota(jnp.int32, (NORM_GROUPS, width), 1)
    inner = jnp.where(lane < used, lane, lane - used)
    upper = pltpu.roll(own, width - crops, 1)
    lower = pltpu.roll(own, crops, 1)
    out_ref[0] = own
    out_ref[1] = jnp.where(inner < crops, upper, jnp.where(inner < 2 * crops, lower, own))
    odd = lax.div(lax.axis_index("rows"), CROP // rows) & 1
    near = jnp.where(inner < crops, odd, jnp.where(inner < 2 * crops, 1 - odd, 1))
    side_ref[0] = near.astype(F32)
    side_ref[1] = jnp.where(inner < 2 * crops, 1 - near, 1).astype(F32)
    for kernel_copy in later:
        kernel_copy.wait()


def strip_statistics(strip, crop_shift, local_kernel, global_kernel, dil_rows):
    rows, channels, columns = strip.shape
    crops, used, width = lane_plan(columns, dil_rows)
    edge = jax.ShapeDtypeStruct((dil_rows, channels, columns), BF16)
    kernel = jax.ShapeDtypeStruct(local_kernel.shape, BF16)
    vmem = pl.BlockSpec(memory_space=pltpu.VMEM)
    return pl.pallas_call(
        functools.partial(stats_body, dil_rows, channels // NORM_GROUPS),
        out_shape=(
            jax.ShapeDtypeStruct((2, NORM_GROUPS, width), F32),
            edge,
            edge,
            kernel,
            kernel,
            jax.ShapeDtypeStruct(strip.shape, BF16),
            jax.ShapeDtypeStruct((2, NORM_GROUPS, width), F32),
        ),
        in_specs=[pl.BlockSpec(memory_space=pltpu.HBM)] * 4,
        out_specs=(vmem,) * 7,
        scratch_shapes=[
            pltpu.SMEM(crop_shift.shape, jnp.int32),
            pltpu.VMEM((2, dil_rows, 2 * columns, width), BF16),
            pltpu.SemaphoreType.DMA(()),
            pltpu.SemaphoreType.DMA((3,)),
        ],
        compiler_params=pltpu.CompilerParams(vmem_limit_bytes=16 << 20),
        cost_estimate=pl.CostEstimate(
            flops=12 * strip.size, bytes_accessed=2 * strip.size, transcendentals=0
        ),
        name="strip_statistics",
    )(in_hbm(crop_shift), in_hbm(strip), in_hbm(local_kernel), in_hbm(global_kernel))


def pack_body(local_ref, global_ref, *refs):
    vectors, (weight_out, affine_out, rows, sems) = refs[:-4], refs[-4:]
    channels = local_ref.shape[2]
    copies = []
    for i, vector in enumerate(vectors):
        copy = pltpu.make_async_copy(vector, rows.at[i], sems.at[i])
        copy.start()
        copies.append(copy)
    taps = [ref[t // 3, t % 3] for ref in (local_ref, global_ref) for t in range(9)]
    stacked = jnp.concatenate(taps, axis=0)
    for start in range(0, stacked.shape[0], LANES):
        weight_out[:, start : start + LANES] = stacked[start : start + LANES].T
    for copy in copies:
        copy.wait()
    table = [rows[i].reshape(1, channels) for i in range(len(vectors))]
    table.append(jnp.zeros((LANES - len(vectors), channels), F32))
    affine_out[...] = jnp.concatenate(table, axis=0).T


def pack_parameters(local_kernel, global_kernel, vectors):
    channels = local_kernel.shape[2]
    vmem = pl.BlockSpec(memory_space=pltpu.VMEM)
    return pl.pallas_call(
        pack_body,
        out_shape=(
            jax.ShapeDtypeStruct((channels, 18 * channels), BF16),
            jax.ShapeDtypeStruct((channels, LANES), F32),
        ),
        in_specs=[vmem] * 2 + [pl.BlockSpec(memory_space=pltpu.HBM)] * len(vectors),
        out_specs=(vmem, vmem),
        scratch_shapes=[
            pltpu.VMEM((len(vectors), channels), F32),
            pltpu.SemaphoreType.DMA((len(vectors),)),
        ],
        compiler_params=pltpu.CompilerParams(vmem_limit_bytes=12 << 20),
        cost_estimate=pl.CostEstimate(
            flops=0, bytes_accessed=8 * local_kernel.size, transcendentals=0
        ),
        name="pack_parameters",
    )(local_kernel, global_kernel, *[in_hbm(vector) for vector in vectors])


def main_body(
    dil_rows,
    group_size,
    image_cells,
    crop_shift,
    dilation_shift,
    x_ref,
    pair_ref,
    other_ref,
    total_ref,
    affine_ref,
    weight_ref,
    out_ref,
    crop_coef,
    image_coef,
    operand_ref,
    out_buf,
    out_sem,
):
    rows, channels, columns = x_ref.shape
    crops, used, width = lane_plan(columns, dil_rows)
    coef_lanes = -(-3 * used // LANES) * LANES
    sub_cols = columns // DILATION_COLUMNS
    first = lax.axis_index("rows") * rows
    sub_rows = image_cells // sub_cols
    split_row = split_of_strip(crop_shift[0], rows)
    split_col = jnp.remainder(crop_shift[1], CROP)
    image_row = jnp.remainder(dilation_shift[0], sub_rows)
    image_col = jnp.remainder(dilation_shift[1], sub_cols)

    def local_valid(row):
        return jnp.remainder(first + row - jnp.remainder(crop_shift[0], CROP) + CROP, CROP) != 0

    def global_valid(row):
        place = lax.div(first + row, dil_rows) - image_row + sub_rows
        return jnp.remainder(place, sub_rows) != 0

    lane = lax.broadcasted_iota(jnp.int32, (NORM_GROUPS, width), 1)
    inner = jnp.where(lane < used, lane, lane - used)
    total = total_ref[...]
    count = jnp.where(inner < 2 * crops, CROP * CROP * group_size, image_cells * group_size)
    average = total / count.astype(F32)
    square = pltpu.roll(average, width - used, 1)
    inverse = lax.rsqrt(jnp.maximum(square - average * average, 0.0) + EPSILON)
    moments = jnp.where(lane < used, average, pltpu.roll(inverse, used, 1))
    moments = jnp.where(lane < 2 * used, moments, 0.0)
    groups = group_selector((channels, 3 * NORM_GROUPS), 0, group_size)
    spread = jnp.dot(
        groups, jnp.concatenate(split3(moments), axis=0), preferred_element_type=F32
    )
    lane = lax.broadcasted_iota(jnp.int32, (channels, width), 1)
    at_crop = lane < 2 * crops
    gain = jnp.where(at_crop, affine_ref[:, 0:1], affine_ref[:, 2:3]) * 0.5
    bias = jnp.where(at_crop, affine_ref[:, 1:2], affine_ref[:, 3:4]) * 0.5
    scale = pltpu.roll(spread, width - used, 1) * gain
    shift = bias - spread * scale
    packed = []
    for value in (scale, shift):
        high, middle, low = split3(jnp.where(lane < used, value, 0.0))
        parts = [high.astype(F32), middle.astype(F32), low.astype(F32)]
        pad = coef_lanes - width
        if pad:
            parts = [
                jnp.concatenate([part, jnp.zeros((channels, pad), F32)], axis=1) for part in parts
            ]
        whole = parts[0] + pltpu.roll(parts[1], used, 1) + pltpu.roll(parts[2], 2 * used, 1)
        packed.append(whole.astype(BF16))
    selector_lane = lax.broadcasted_iota(jnp.int32, (coef_lanes, columns), 0)
    column = lax.broadcasted_iota(jnp.int32, (coef_lanes, columns), 1)
    selector_lane = jnp.where(
        selector_lane < used,
        selector_lane,
        jnp.where(
            selector_lane < 2 * used,
            selector_lane - used,
            jnp.where(selector_lane < 3 * used, selector_lane - 2 * used, width),
        ),
    )
    crop = crop_of(column, split_col, columns)
    chosen = [one_hot(selector_lane == crop + slot * crops) for slot in range(2)]
    phase = (column & (DILATION_COLUMNS - 1))[:, :LANES]
    for p in range(dil_rows):
        chosen.append(
            one_hot(selector_lane[:, :LANES] == phase + 2 * crops + p * DILATION_COLUMNS)
        )
    chosen = jnp.concatenate(chosen, axis=1)
    for k in range(2):
        table = jnp.dot(packed[k], chosen, preferred_element_type=F32)
        for slot in range(2):
            crop_coef[slot, k] = table[:, slot * columns : (slot + 1) * columns]
        for p in range(dil_rows):
            start = 2 * columns + p * LANES
            image_coef[p, k] = table[:, start : start + LANES]

    column = lax.broadcasted_iota(jnp.int32, (16, columns), 1)
    crop_col = (column - split_col) & (CROP - 1)
    image_q = (lax.shift_right_logical(column, 3) - image_col) & (sub_cols - 1)
    crop_left = one_hot(crop_col != 0)[:1]
    crop_right = one_hot(crop_col != CROP - 1)[:1]
    image_left = one_hot(image_q != 0)[:1]
    image_right = one_hot(image_q != sub_cols - 1)[:1]

    odd = (lax.axis_index("rows") & 1) == 1

    def source(row):
        if row < 0:
            row += dil_rows
            return jnp.where(odd, pair_ref[row], other_ref[row]).astype(F32)
        if row >= rows:
            row -= rows
            return jnp.where(odd, other_ref[row], pair_ref[row]).astype(F32)
        return x_ref[row].astype(F32)

    def flag(valid):
        return jnp.where(valid, jnp.ones((16, columns), F32), 0.0).astype(BF16)[:1]

    def spread(base, row, step, shift, half, mask_left, mask_right, valid):
        act = (half + half * jnp.tanh(half)).astype(BF16)
        from_left = pltpu.roll(act, shift, 1)
        from_right = pltpu.roll(act, columns - shift, 1)
        for tap, target in ((0, row + step), (1, row), (2, row - step)):
            if not 0 <= target < rows:
                continue
            start = base + tap * 3 * channels
            left, centre, right = mask_left, act, mask_right
            if tap != 1:
                counts = flag(valid(target if tap == 0 else row))
                left, centre, right = left * counts, act * counts, right * counts
            operand_ref[target, start : start + channels] = from_left * left
            operand_ref[target, start + channels : start + 2 * channels] = centre
            operand_ref[target, start + 2 * channels : start + 3 * channels] = from_right * right

    def local_row(row):
        slot = jnp.where(min(max(row, 0), rows - 1) < split_row, 0, 1)
        half = source(row) * crop_coef[slot, 0] + crop_coef[slot, 1]
        spread(0, row, 1, 1, half, crop_left, crop_right, local_valid)

    def global_row(row):
        scale, shift = image_coef[row % dil_rows, 0], image_coef[row % dil_rows, 1]
        value = source(row)
        half = jnp.concatenate(
            [
                value[:, start : start + LANES] * scale + shift
                for start in range(0, columns, LANES)
            ],
            axis=1,
        )
        base = 9 * channels
        spread(
            base, row, dil_rows, DILATION_COLUMNS, half, image_left, image_right, global_valid
        )

    offset = affine_ref[:, 4:5] + affine_ref[:, 5:6]
    done_local = -1
    done_global = -dil_rows
    copies = []
    for base in range(0, rows, 2):
        while done_local <= base + 2:
            local_row(done_local)
            done_local += 1
        while done_global <= base + 1 + dil_rows:
            global_row(done_global)
            done_global += 1
        operand = jnp.concatenate([operand_ref[base], operand_ref[base + 1]], axis=1)
        result = jnp.dot(weight_ref[...], operand, preferred_element_type=F32)
        for row in range(base, base + 2):
            part = result[:, (row - base) * columns : (row - base + 1) * columns]
            out_buf[row] = (part + offset).astype(BF16)
            copy = pltpu.make_async_copy(out_buf.at[row], out_ref.at[row], out_sem.at[row])
            copy.start()
            copies.append(copy)
    for copy in copies:
        copy.wait()


def main_call(
    strip, pair, other, totals, affine, weights, crop_shift, dilation_shift
):
    rows, channels, columns = strip.shape
    dil_rows = pair.shape[0]
    smem = pl.BlockSpec(memory_space=pltpu.SMEM)
    vmem = pl.BlockSpec(memory_space=pltpu.VMEM)
    image_cells = (rows * lax.axis_size("rows") // dil_rows) * (columns // DILATION_COLUMNS)
    return pl.pallas_call(
        functools.partial(main_body, dil_rows, channels // NORM_GROUPS, image_cells),
        out_shape=jax.ShapeDtypeStruct(strip.shape, BF16),
        in_specs=[smem, smem] + [vmem] * 6,
        out_specs=pl.BlockSpec(memory_space=pl.ANY),
        scratch_shapes=[
            pltpu.VMEM((2, 2, channels, columns), F32),
            pltpu.VMEM((dil_rows, 2, channels, LANES), F32),
            pltpu.VMEM((rows, 18 * channels, columns), BF16),
            pltpu.VMEM(strip.shape, BF16),
            pltpu.SemaphoreType.DMA((rows,)),
        ],
        compiler_params=pltpu.CompilerParams(vmem_limit_bytes=40 << 20),
        cost_estimate=pl.CostEstimate(
            flops=36 * channels * strip.size,
            bytes_accessed=4 * strip.size,
            transcendentals=2 * strip.size,
        ),
        name="crop_and_dilated",
    )(crop_shift, dilation_shift, strip, pair, other, totals, affine, weights)


def shards(
    latent,
    crop_shift,
    dilation_shift,
    local_gain,
    local_bias,
    local_kernel,
    local_offset,
    global_gain,
    global_bias,
    global_kernel,
    global_offset,
):
    rows, columns, channels = latent.shape
    devices = lax.axis_size("rows")
    dil_rows = devices // DILATION_COLUMNS
    strip = latent.transpose(0, 2, 1)

    def shifted(value, step):
        return lax.ppermute(value, "rows", [(i, (i + step) % devices) for i in range(devices)])

    def exchanged(value, bit):
        return lax.ppermute(value, "rows", [(i, i ^ bit) for i in range(devices)])

    def paired(value, start):
        links = [(i % devices, (i + 1) % devices) for i in range(start, devices + start, 2)]
        return lax.ppermute(value, "rows", links + [(b, a) for a, b in links])

    totals, pair, other, local_kernel, global_kernel, strip, side = strip_statistics(
        strip, crop_shift, local_kernel, global_kernel, dil_rows
    )
    pair = paired(pair, 0)
    other = paired(other, 1)
    span = CROP // rows
    totals = totals + exchanged(totals, 1)
    own, swapped = totals[0], totals[1]
    crops, used, width = lane_plan(columns, dil_rows)
    inner = jnp.arange(width, dtype=jnp.int32)
    inner = jnp.where(inner < used, inner, inner - used)
    if devices == 4 * span:
        near = exchanged(swapped, span)
        across = exchanged(swapped, 2 * span)
        third = exchanged(swapped, 3 * span)
        totals = (own + side[0] * near) + side[1] * third
        totals = totals + jnp.where(inner < 2 * crops, 0.0, across)
    else:
        above = shifted(swapped, span)
        below = shifted(swapped, -span)
        image = own
        bit = span
        while bit < devices:
            image = image + exchanged(image, bit)
            bit *= 2
        totals = own + jnp.where(inner < crops, above, below)
        totals = jnp.where(inner < 2 * crops, totals, image)
    totals, local_kernel = lax.optimization_barrier((totals, local_kernel))
    bit = 2
    while bit < span:
        totals = totals + exchanged(totals, bit)
        bit *= 2
    vectors = (local_gain, local_bias, global_gain, global_bias, local_offset, global_offset)
    weights, affine = pack_parameters(local_kernel, global_kernel, vectors)
    result = main_call(
        strip, pair, other, totals, affine, weights, crop_shift, dilation_shift
    )
    return result.transpose(0, 2, 1)


def solution(mesh):
    return jax.shard_map(
        shards,
        mesh=mesh,
        in_specs=(
            P(("groups", "rows"), None, None),
            P("groups"),
            P("groups"),
            P(),
            P(),
            P(),
            P(),
            P(),
            P(),
            P(),
            P(),
        ),
        out_specs=P(("groups", "rows"), None, None),
        check_vma=False,
    )
```
